32 devices in a mesh: row: 4 (over x, core), col: 8 (over z, y).
Axes of the slice: x: 2, y: 2, z: 4, core: 2. Of those that a mesh axis runs over, the one named last changes fastest.
Arguments:
- item_ids: int32 [8192], P(('row', 'col')), may hold values from 0 to 63
- user_lengths: int32 [8], replicated, may hold values from 1 to 2048, 8192 in all
- catalogue: bfloat16 [64, 1024], P(('row', 'col')), may hold values from -6 to 6
- tap_lengths: int32 [1, 1024], replicated, may hold values from 64 to 256
- conv_taps: bfloat16 [1, 256, 1024], replicated, may hold values from -0.375 to 0.375
- norm_gains: float32 [1, 2, 1024], replicated, may hold values from 0.1 to 1.9
- gate_weight: bfloat16 [1, 1024, 1024], P(None, 'col'), may hold values from -0.1875 to 0.1875
- up_weight: bfloat16 [1, 1024, 1024], P(None, 'col'), may hold values from -0.1875 to 0.1875
- down_weight: bfloat16 [1, 1024, 1024], P(None, 'col'), may hold values from -0.1875 to 0.1875
Outputs:
- history_out: bfloat16 [8192, 1024], P(('row', 'col'))
The draws below stay inside these ranges and needn't reach their ends.
Inputs may be any that keep to these rules, and one draw needn't show every extreme that they name: `user_lengths`: the 8 lengths sum to 8192.
All inputs are finite; a program needn't handle non-finite values.
Results may differ from the reference program's by a relative error of at most 0.0054.
Values may be sent and summed in bfloat16 or wider, within the bound.
No kernel may reach another device: no remote copies, remote signals or barrier semaphores. Data moves between devices by JAX's collectives and lax.ppermute only.
A program may use at most 64 MiB of HBM per device.

```python
import math
import jax
import jax.numpy as jnp
import numpy as np
from jax import lax

D = 1024
FF = 1024
K = 256
LAYERS = 1
TOK_DEV = 256
TOKENS = 8192
ITEMS = 64
USERS = 8
N_ROW = 4


def set_ends(entries, own_key, least, largest):
    longest = entries.shape.index(max(entries.shape))
    spots = []
    for shift in (0, 1):
        where = [jax.random.randint(jax.random.fold_in(own_key, axis), (), 0, length) for axis, length in enumerate(entries.shape)]
        where[longest] = (where[longest] + shift) % entries.shape[longest]
        spots.append(tuple(where))
    return entries.at[spots[0]].set(least).at[spots[1]].set(largest)


def steps_of(own_key, extent, shards, least, largest):
    gain = 1.0
    for position, blocks in shards:
        steps = jax.random.uniform(jax.random.fold_in(jax.random.fold_in(own_key, 6), position), (blocks,), jnp.float32, least / len(shards), largest / len(shards))
        gain = gain * jnp.repeat(jnp.exp(steps), extent[position] // blocks).reshape((-1,) + (1,) * (len(extent) - 1 - position))
    return gain


def cumulative_ranks(count, slope):
    loads = [(1 << 20) // math.isqrt(grade ** slope) + 1 for grade in range(1, count + 1)]
    deviation = 1 + sum(loads) // (1 << 30)
    return np.cumsum(np.array([max(1, weight // deviation) for weight in loads]))


def ranked_ids(key, dims, number_of, slope):
    grid = cumulative_ranks(number_of, slope)
    ticket = jax.random.randint(jax.random.fold_in(key, 1), dims, 0, int(grid[number_of - 1]))
    standing = jnp.searchsorted(jnp.asarray(grid, jnp.int32), ticket, side="right")
    return jax.random.permutation(jax.random.fold_in(key, 2), number_of)[standing].astype(jnp.int32)


def profile(amount, total, bound, lean):
    loads = [(1 << 20) // math.isqrt(grade ** lean) + 1 for grade in range(2, amount + 1)]
    spare, counts = total - bound - (amount - 1), [1] * (amount - 1)
    while spare > 0:
        movable = [i for i in range(amount - 1) if counts[i] < bound]
        whole, left = sum([loads[i] for i in movable]), spare
        for i in movable:
            more = min(bound - counts[i], max(1, left * loads[i] // whole), spare)
            counts[i] = counts[i] + more
            spare = spare - more
    return np.array([bound] + counts)


def ragged_sizes(own_key, amount, total, reach, slope):
    if amount == 2:
        one = jax.random.randint(own_key, (), max(1, total - reach), min(reach, total - 1) + 1)
        return jnp.stack([one, total - one])
    lengths = jnp.asarray(profile(amount, total, reach, slope), jnp.int32)
    twos = (amount - 1) // 2
    source_of, sink = lengths[1:1 + 2 * twos:2], lengths[2:2 + 2 * twos:2]
    slack = jnp.minimum(source_of - 1, reach - sink)
    passed = jax.random.randint(jax.random.fold_in(own_key, 1), (twos,), 0, 1 << 20) % (slack + 1)
    lengths = lengths.at[1:1 + 2 * twos:2].set(source_of - passed).at[2:2 + 2 * twos:2].set(sink + passed)
    return lengths[jax.random.permutation(jax.random.fold_in(own_key, 2), amount)]


def normal_values(key, shape, spread, bound, shards=(), kind=jnp.bfloat16):
    entries = spread * jax.random.normal(key, shape, jnp.float32)
    if shards:
        entries = entries * steps_of(key, shape, shards, -0.22, 0.18)
    return jnp.clip(entries, -bound, bound).astype(kind)


def setup_inputs(seed: int = 0) -> dict:
    key_list = jax.random.split(jax.random.key(seed), 10)
    item_ids = set_ends(ranked_ids(key_list[0], (TOKENS,), ITEMS, 2), jax.random.fold_in(key_list[0], 3), 0, ITEMS - 1).astype(jnp.int32)
    user_lengths = ragged_sizes(key_list[1], USERS, TOKENS, TOKENS // N_ROW, 2).astype(jnp.int32)
    catalogue = normal_values(key_list[2], (ITEMS, D), 1.0, 6.0, ((0, 32),))
    tap_lengths = set_ends(jax.random.randint(key_list[3], (LAYERS, D), K // 4, K + 1), jax.random.fold_in(key_list[3], 1), K // 4, K).astype(jnp.int32)
    conv_taps = normal_values(key_list[4], (LAYERS, K, D), K ** -0.5, 0.375)
    norm_gains = jnp.clip(1.0 + 0.18 * jax.random.normal(key_list[5], (LAYERS, 2, D), jnp.float32), 0.1, 1.9)
    gate_weight = normal_values(key_list[6], (LAYERS, D, FF), D ** -0.5, 0.1875, ((1, 8),))
    up_weight = normal_values(key_list[7], (LAYERS, D, FF), D ** -0.5, 0.1875, ((1, 8),))
    down_weight = normal_values(key_list[8], (LAYERS, FF, D), FF ** -0.5, 0.1875, ((1, 8),))
    return dict(item_ids=item_ids, user_lengths=user_lengths, catalogue=catalogue, tap_lengths=tap_lengths, conv_taps=conv_taps, norm_gains=norm_gains, gate_weight=gate_weight, up_weight=up_weight, down_weight=down_weight)


epsilon = 1e-06

def rms_norm(values, gains):
    scale = lax.rsqrt(lax.optimization_barrier(jnp.mean(values * values, axis=-1, keepdims=True)) + epsilon)
    return values * scale * gains

def token_ages(positions, user_starts):
    reached = user_starts[None, :] <= positions[:, None]
    fallback = jnp.minimum(positions, 0)[:, None]
    seg_start = lax.optimization_barrier(jnp.max(jnp.where(reached, user_starts[None, :], fallback), axis=1))
    return positions - seg_start

def reference(item_ids, user_lengths, catalogue, tap_lengths, conv_taps, norm_gains, gate_weight, up_weight, down_weight):
    hidden = jnp.take(catalogue, item_ids, axis=0).astype(jnp.float32)
    positions = jnp.arange(TOKENS, dtype=jnp.int32)
    user_starts = (jnp.cumsum(user_lengths) - user_lengths).astype(jnp.int32)
    token_age = token_ages(positions, user_starts)
    lag_column = jnp.arange(K, dtype=jnp.int32)[:, None]
    block_count = TOKENS // TOK_DEV
    for layer_index in range(LAYERS):
        normed = rms_norm(hidden, norm_gains[layer_index, 0]).astype(jnp.bfloat16)
        tap_table = conv_taps[layer_index].astype(jnp.float32) * (lag_column < tap_lengths[layer_index][None, :]).astype(jnp.float32)
        padded = jnp.concatenate([jnp.zeros((K - 1, D), jnp.bfloat16), normed], axis=0)
        gains_inner = norm_gains[layer_index, 1]
        gate_now = gate_weight[layer_index]
        up_now = up_weight[layer_index]
        down_now = down_weight[layer_index]

        def one_block(block_index):
            start = (block_index * TOK_DEV).astype(jnp.int32)
            extended = lax.dynamic_slice_in_dim(padded, start, TOK_DEV + K - 1, 0)
            ages = lax.dynamic_slice_in_dim(token_age, start, TOK_DEV, 0)
            rows = lax.dynamic_slice_in_dim(hidden, start, TOK_DEV, 0)

            def add_lag(lag_index, accumulated):
                begin = (K - 1 - lag_index).astype(jnp.int32)
                shifted = lax.dynamic_slice_in_dim(extended, begin, TOK_DEV, 0)
                weights = lax.dynamic_slice_in_dim(tap_table, jnp.asarray(lag_index).astype(jnp.int32), 1, 0)
                keep = (lag_index <= ages)[:, None]
                return accumulated + jnp.where(keep, shifted.astype(jnp.float32) * weights, 0.0)
            mixing = lax.fori_loop(0, K, add_lag, jnp.zeros((TOK_DEV, D), jnp.float32))
            rows = rows + mixing
            inner = rms_norm(rows, gains_inner).astype(jnp.bfloat16)
            gate_sum = jnp.dot(inner, gate_now, preferred_element_type=jnp.float32)
            up_sum = jnp.dot(inner, up_now, preferred_element_type=jnp.float32)
            activated = (jax.nn.silu(gate_sum) * up_sum).astype(jnp.bfloat16)
            return rows + jnp.dot(activated, down_now, preferred_element_type=jnp.float32)
        blocks = lax.map(one_block, jnp.arange(block_count, dtype=jnp.int32))
        hidden = blocks.reshape(TOKENS, D)
    return hidden.astype(jnp.bfloat16)
```

```python
import functools

import jax
import jax.numpy as jnp
import numpy as np
from jax import lax
from jax.experimental import pallas as pl
from jax.experimental.pallas import tpu as pltpu
from jax.sharding import PartitionSpec as P

epsilon = 1e-06
lane_chunk = 256
both = ("row", "col")


def split_bf16(table):
    high = table.astype(jnp.bfloat16)
    low = (table - high.astype(np.float64)).astype(jnp.bfloat16)
    return high, low


def transform_tables(window, out_rows):
    half = window // 2
    angle = 2 * np.pi * np.outer(np.arange(half) + 0.5, np.arange(window)) / window
    forward = np.concatenate([np.cos(angle), np.sin(angle)], axis=0)
    inverse = forward[:, window - out_rows :].T * (2.0 / window)
    return split_bf16(forward), split_bf16(inverse)


def dot(a, b):
    return jnp.dot(a, b, preferred_element_type=jnp.float32)


def whole(memory_space=pltpu.VMEM):
    return pl.BlockSpec(memory_space=memory_space)


def taps_kernel(taps, lengths, f_high, f_low, spectrum):
    count = taps.shape[0]
    lag = lax.broadcasted_iota(jnp.int32, (count, lane_chunk), 0)
    for start in range(0, taps.shape[1], lane_chunk):
        cols = pl.ds(start, lane_chunk)
        kept = jnp.where(lag < lengths[:, cols], taps[:, cols].astype(jnp.float32), 0.0)
        kept = kept.astype(jnp.bfloat16)
        spectrum[:, cols] = dot(f_high[:, :count], kept) + dot(f_low[:, :count], kept)


def taps_spectrum(taps, lengths, f_high, f_low):
    window, width = f_high.shape[0], taps.shape[1]
    return pl.pallas_call(
        taps_kernel,
        out_shape=jax.ShapeDtypeStruct((window, width), jnp.float32),
        in_specs=[whole()] * 4,
        out_specs=whole(),
        name="taps",
        cost_estimate=pl.CostEstimate(
            flops=4 * window * taps.shape[0] * width, bytes_accessed=5 << 20, transcendentals=0
        ),
    )(taps, lengths, f_high, f_low)


def mix_kernel(lengths, before, own, table, gains, spectrum, f_high, f_low, g_high, g_low,
               hidden, inner, normed, chosen):
    items, width = table.shape
    count = own.shape[1]
    window = 2 * count
    half = window // 2
    first = (lax.axis_index("row") * lax.axis_size("col") + lax.axis_index("col")) * count

    rows = table[...].astype(jnp.float32)
    scale = lax.rsqrt(jnp.mean(rows * rows, axis=-1, keepdims=True) + epsilon)
    normed[...] = (rows * scale * gains[0:1, :]).astype(jnp.bfloat16)
    ids = jnp.concatenate([before[...], own[...]], axis=1)
    hit = lax.broadcasted_iota(jnp.int32, (items, window), 0) == ids
    chosen[...] = jnp.where(hit, 1.0, 0.0).T.astype(jnp.bfloat16)
    for start in range(0, width, lane_chunk):
        cols = pl.ds(start, lane_chunk)
        hidden[:, cols] = dot(chosen[count:, :], table[:, cols])

    at = lax.broadcasted_iota(jnp.int32, (window, 1), 0) + (first - count)

    def one_user(user, begin):
        end = begin + lengths[user]

        @pl.when(jnp.logical_and(begin < first + count, end > first))
        def _():
            inside = jnp.logical_and(at >= begin, at < end)
            picked = jnp.where(inside, chosen[...].astype(jnp.float32), 0.0).astype(jnp.bfloat16)

            @pl.loop(0, width // lane_chunk)
            def _(chunk):
                cols = pl.ds(pl.multiple_of(chunk * lane_chunk, lane_chunk), lane_chunk)
                x = dot(picked, normed[:, cols]).astype(jnp.bfloat16)
                seen = dot(f_high[...], x) + dot(f_low[...], x)
                x_cos, x_sin = seen[:half], seen[half:]
                w_cos, w_sin = spectrum[:half, cols], spectrum[half:, cols]
                y = jnp.concatenate(
                    [x_cos * w_cos - x_sin * w_sin, x_cos * w_sin + x_sin * w_cos], axis=0
                )
                y_high = y.astype(jnp.bfloat16)
                y_low = (y - y_high.astype(jnp.float32)).astype(jnp.bfloat16)
                mixed = dot(g_high[...], y_high) + dot(g_high[...], y_low) + dot(g_low[...], y_high)
                hidden[:, cols] += jnp.where(inside[count:], mixed, 0.0)

        return end

    lax.fori_loop(0, lengths.shape[0], one_user, jnp.int32(0))
    mixed = hidden[...]
    scale = lax.rsqrt(jnp.mean(mixed * mixed, axis=-1, keepdims=True) + epsilon)
    inner[...] = (mixed * scale * gains[1:2, :]).astype(jnp.bfloat16)


def mix(lengths, before, own, table, gains, spectrum, forward, inverse):
    count, (items, width) = own.shape[1], table.shape
    return pl.pallas_call(
        mix_kernel,
        out_shape=(
            jax.ShapeDtypeStruct((count, width), jnp.float32),
            jax.ShapeDtypeStruct((count, width), jnp.bfloat16),
        ),
        in_specs=[whole(pltpu.SMEM)] + [whole()] * 9,
        out_specs=(whole(), whole()),
        scratch_shapes=[
            pltpu.VMEM((items, width), jnp.bfloat16),
            pltpu.VMEM((2 * count, items), jnp.bfloat16),
        ],
        name="mix",
        cost_estimate=pl.CostEstimate(
            flops=2 * width * count * count * 16, bytes_accessed=8 << 20, transcendentals=0
        ),
    )(lengths, before, own, table, gains, spectrum, *forward, *inverse)


def feed_kernel(plan, *refs):
    inner, hidden = refs[:2]
    pieces, (out, gate, up, down, active, sems) = refs[2:-6], refs[-6:]
    always, in_middle, at_ends, middle = plan(pieces, (gate, up, down), sems)

    def on_all(action):
        for copy in always:
            action(copy)
        if middle is not None:
            pl.when(middle)(lambda: [action(copy) for copy in in_middle] and None)
            pl.when(jnp.logical_not(middle))(lambda: [action(copy) for copy in at_ends] and None)

    on_all(lambda copy: copy.start())
    on_all(lambda copy: copy.wait())
    width, inside = gate.shape[0], gate.shape[1]

    @pl.loop(0, inside // lane_chunk)
    def _(chunk):
        cols = pl.ds(pl.multiple_of(chunk * lane_chunk, lane_chunk), lane_chunk)
        gate_sum = dot(inner[...], gate[:, cols])
        up_sum = dot(inner[...], up[:, cols])
        active[:, cols] = (gate_sum / (1.0 + jnp.exp(-gate_sum)) * up_sum).astype(jnp.bfloat16)

    @pl.loop(0, width // lane_chunk)
    def _(chunk):
        cols = pl.ds(pl.multiple_of(chunk * lane_chunk, lane_chunk), lane_chunk)
        out[:, cols] = (hidden[:, cols] + dot(active[...], down[:, cols])).astype(jnp.bfloat16)


def feed(inner, hidden, pieces, plan, copies, width, inside):
    count = inner.shape[0]
    return pl.pallas_call(
        functools.partial(feed_kernel, plan),
        out_shape=jax.ShapeDtypeStruct((count, width), jnp.bfloat16),
        in_specs=[whole(), whole()] + [whole(pl.ANY)] * len(pieces),
        out_specs=whole(),
        scratch_shapes=[
            pltpu.VMEM((width, inside), jnp.bfloat16),
            pltpu.VMEM((width, inside), jnp.bfloat16),
            pltpu.VMEM((inside, width), jnp.bfloat16),
            pltpu.VMEM((count, inside), jnp.bfloat16),
            pltpu.SemaphoreType.DMA((copies,)),
        ],
        name="feed",
        cost_estimate=pl.CostEstimate(
            flops=6 * count * width * inside, bytes_accessed=8 << 20, transcendentals=count * inside
        ),
    )(inner, hidden, *pieces)


def col_route(lane, place):
    size = lax.axis_size("col")
    pairs = []
    for device in range(size):
        target = place(device // 2)
        if target is not None:
            pairs.append((device, target * 2 + (device % 2 ^ lane)))
    return pairs


def partner(block):
    return lax.ppermute(block, "row", [(i, i ^ 1) for i in range(lax.axis_size("row"))])


def travel(weights):
    core = lax.axis_index("row") % 2
    place = lax.axis_index("col") // 2
    middle = jnp.logical_or(place == 1, place == 2)
    half = weights[0].shape[0] // 2
    own = jnp.concatenate(
        [lax.dynamic_slice_in_dim(w, core * half, half, 0) for w in weights], axis=0
    )
    cross = lambda p: None if p in (0, 3) else 3 - p
    side = lambda p: p ^ 1
    outward = lambda p: {1: 0, 2: 3}.get(p)
    stay = lambda p: p
    ends = lambda p: p if p in (0, 3) else None
    send = lambda block, lane, where: lax.ppermute(block, "col", col_route(lane, where))

    across = send(own, 1, stay)
    beside = send(own, 0, side)
    inward = send(own, 0, cross)
    second = send(jnp.where(middle, inward, across), 0, side)
    far = send(beside, 0, cross)
    other = send(jnp.where(middle, inward, beside), 1, stay)
    last = send(far, 0, outward)
    size = lax.axis_size("col")
    turn = [(d, (3 - d // 2) * 2 + d % 2) if d // 2 in (1, 2) else (d, d ^ 1) for d in range(size)]
    third = lax.ppermute(second, "col", turn)
    cut = third.shape[0] // 2
    top = send(third[:cut], 0, outward)
    bottom = send(last[cut:], 1, ends)
    mine = [across, beside, inward, second, far, other, last, third, top, bottom]
    return mine, [partner(block) for block in mine]


def travel_plan(pieces, buffers, sems):
    core = lax.axis_index("row") % 2
    col = lax.axis_index("col")
    lane, place = col % 2, col // 2
    beside = jnp.where(place % 2 == 0, place + 1, place - 1)
    shares, mine, theirs = pieces[:3], pieces[3:13], pieces[13:23]
    depth = shares[0].shape[0]
    half = depth // 2
    middle = jnp.logical_or(place == 1, place == 2)
    used = iter(range(sems.shape[0]))

    def put(source, buffer, row, rows):
        where = buffer.at[pl.ds(pl.multiple_of(row, rows), rows)]
        return pltpu.make_async_copy(source, where, sems.at[next(used)])

    always = [put(w, buffer, col * depth, depth) for w, buffer in zip(shares, buffers)]
    inside, outside = [], []
    for got, part in ((mine, core), (theirs, 1 - core)):
        across, side, inward, second, far, other, last, third, top, bottom = got

        def at(other_place, other_lane):
            return (other_place * 2 + other_lane) * depth + part * half

        def full(piece, row):
            return [
                put(piece.at[pl.ds(i * half, half)], buffer, row, half)
                for i, buffer in enumerate(buffers)
            ]

        always += full(across, at(place, 1 - lane))
        always += full(side, at(beside, lane))
        always += full(third, at(3 - beside, 1 - lane))
        always += full(
            second,
            jnp.where(middle, at(beside, 1 - lane), at(3 - beside, lane)),
        )
        always += full(other, at(jnp.where(middle, 3 - place, beside), 1 - lane))
        inside += full(inward, at(3 - place, lane)) + full(far, at(3 - beside, lane))
        outside += full(last, at(3 - place, lane))
        row, cut = at(3 - place, 1 - lane), half // 2
        gate, up, down = buffers
        outside.append(put(top.at[pl.ds(0, half)], gate, row, half))
        outside.append(put(top.at[pl.ds(half, cut)], up, row, cut))
        outside.append(put(bottom.at[pl.ds(0, cut)], up, row + cut, cut))
        outside.append(put(bottom.at[pl.ds(cut, half)], down, row, half))
    return always, inside, outside, middle


def gathered_plan(pieces, buffers, sems):
    copies = [
        pltpu.make_async_copy(piece, buffer, sems.at[i])
        for i, (piece, buffer) in enumerate(zip(pieces, buffers))
    ]
    return copies, [], [], None


def spread(table):
    devices = lax.axis_size("row") * lax.axis_size("col")
    copies = jnp.broadcast_to(table[None], (devices,) + table.shape)
    rows = lax.all_to_all(copies, both, 0, 0)
    return rows.reshape(devices * table.shape[0], table.shape[1])


def body(item_ids, user_lengths, catalogue, tap_lengths, conv_taps, norm_gains,
         gate_weight, up_weight, down_weight):
    count, width = item_ids.shape[0], catalogue.shape[1]
    shares = [gate_weight[0], up_weight[0], down_weight[0]]
    inside = gate_weight.shape[2]
    if lax.axis_size("col") == 8 and lax.axis_size("row") % 2 == 0:
        mine, theirs = travel(shares)
        pieces, plan, copies = shares + mine + theirs, travel_plan, 64
    else:
        pieces = [lax.all_gather(w, "col", axis=0, tiled=True) for w in shares]
        plan, copies = gathered_plan, 3
    devices = lax.axis_size("row") * lax.axis_size("col")
    before = lax.ppermute(item_ids, both, [(i, i + 1) for i in range(devices - 1)])
    table = spread(catalogue)
    forward, inverse = transform_tables(2 * count, count)
    spectrum = taps_spectrum(conv_taps[0], tap_lengths, *forward)
    hidden, inner = mix(
        user_lengths, before[None], item_ids[None], table, norm_gains[0], spectrum, forward, inverse
    )
    return feed(inner, hidden, pieces, plan, copies, width, inside)


def solution(mesh):
    by_device = P(both)
    by_col = P(None, "col", None)
    return jax.shard_map(
        body,
        mesh=mesh,
        in_specs=(by_device, P(), P(both, None), P(), P(), P(), by_col, by_col, by_col),
        out_specs=P(both, None),
        check_vma=False,
    )
```

```python
import functools

import jax
import jax.numpy as jnp
import numpy as np
from jax import lax
from jax.experimental import pallas as pl
from jax.experimental.pallas import tpu as pltpu
from jax.sharding import PartitionSpec as P

epsilon = 1e-06
lane_chunk = 256
both = ("row", "col")
id_base = 256


def split_bf16(table):
    high = table.astype(jnp.bfloat16)
    low = (table - high.astype(np.float64)).astype(jnp.bfloat16)
    return high, low


def transform_tables(window, out_rows):
    half = window // 2
    angle = 2 * np.pi * np.outer(np.arange(half) + 0.5, np.arange(window)) / window
    forward = np.concatenate([np.cos(angle), np.sin(angle)], axis=0)
    inverse = forward[:, window - out_rows :].T * (2.0 / window)
    return np.concatenate([*split_bf16(forward), *split_bf16(inverse)], axis=0)


def parts_of(tables):
    window = tables.shape[1]
    count = (tables.shape[0] - 2 * window) // 2
    stops = (0, window, 2 * window, 2 * window + count, 2 * window + 2 * count)
    return [tables.at[pl.ds(a, b - a)] for a, b in zip(stops, stops[1:])]


def dot(a, b):
    return jnp.dot(a, b, preferred_element_type=jnp.float32)


def whole(memory_space=pltpu.VMEM):
    return pl.BlockSpec(memory_space=memory_space)


def shape(rows, width, dtype=jnp.bfloat16):
    return jax.ShapeDtypeStruct((rows, width), dtype)


def far(arrays):
    return [pltpu.with_memory_space_constraint(a, pltpu.HBM) for a in arrays]


def call(kernel, out_shape, in_specs, flops, nbytes, limit, scratch=()):
    return pl.pallas_call(
        kernel,
        out_shape=out_shape,
        in_specs=in_specs,
        out_specs=jax.tree.map(lambda _: whole(), out_shape),
        scratch_shapes=list(scratch),
        compiler_params=pltpu.CompilerParams(vmem_limit_bytes=limit << 20),
        cost_estimate=pl.CostEstimate(flops=flops, bytes_accessed=nbytes, transcendentals=0),
    )


def fetch(pairs, sems):
    copies = [pltpu.make_async_copy(a, b, sems.at[i]) for i, (a, b) in enumerate(pairs)]
    for copy in copies:
        copy.start()

    def wait(first=0, end=len(copies)):
        for copy in copies[first:end]:
            copy.wait()

    return wait


def pack_kernel(gate, up, down, own, sems):
    core = lax.axis_index("row") % 2
    depth, half = gate.shape[0], own.shape[1]
    cols = pl.ds(pl.multiple_of(core * half, half), half)
    parts = [(w.at[:, cols], own.at[pl.ds(i * depth, depth)]) for i, w in enumerate((gate, up, down))]
    fetch(parts, sems)()


def pack(gate, up, down):
    depth, width = gate.shape
    return call(
        pack_kernel, shape(3 * depth, width // 2), [whole(pltpu.HBM)] * 3, 0, 1 << 20, 4,
        [pltpu.SemaphoreType.DMA((3,))],
    )(*far((gate, up, down)))


def greet_kernel(ids_far, rows_far, out, ids, rows, sems):
    fetch([(ids_far, ids), (rows_far, rows)], sems)()
    _, width = rows.shape
    count = ids.shape[1]
    numbers = ids[...].astype(jnp.float32)
    high = jnp.floor(numbers * (1.0 / id_base))
    digits = [high, numbers - high * id_base]
    rest = jnp.zeros((1, width - 2 * count), jnp.float32)
    line = jnp.concatenate(digits + [rest], axis=1)
    block = jnp.concatenate([rows[...].astype(jnp.float32), line], axis=0).astype(jnp.bfloat16)

    def one(device, carry):
        out[device] = block
        return carry

    lax.fori_loop(0, out.shape[0], one, 0)


def greet(ids, rows):
    devices = lax.axis_size("row") * lax.axis_size("col")
    out = jax.ShapeDtypeStruct((devices, rows.shape[0] + 1, rows.shape[1]), jnp.bfloat16)
    scratch = [
        pltpu.VMEM(ids.shape, ids.dtype),
        pltpu.VMEM(rows.shape, rows.dtype),
        pltpu.SemaphoreType.DMA((2,)),
    ]
    return call(
        greet_kernel, out, [whole(pltpu.HBM)] * 2, 0, 1 << 18, 16, scratch
    )(*far((ids, rows)))


def taps_kernel(*refs):
    kept, (spectrum, *out), (taps, lengths, sems) = refs[2:5], refs[5:9], refs[9:]
    wait = fetch([*zip(refs[:2], (taps, lengths)), *zip(kept, out)], sems)
    count = taps.shape[0]
    lag = lax.broadcasted_iota(jnp.int32, taps.shape, 0)
    wait(0, 2)
    masked = jnp.where(lag < lengths[...], taps[...].astype(jnp.float32), 0.0).astype(jnp.bfloat16)
    wait(2, 3)
    f_high, f_low, _, _ = parts_of(out[0])
    spectrum[...] = dot(f_high[:, :count], masked) + dot(f_low[:, :count], masked)
    wait(3)


def taps_spectrum(taps, lengths, kept):
    window, (count, width) = kept[0].shape[1], taps.shape
    out = [pltpu.VMEM((window, width), jnp.float32)] + [pltpu.VMEM(k.shape, k.dtype) for k in kept]
    scratch = [
        pltpu.VMEM(taps.shape, taps.dtype),
        pltpu.VMEM(lengths.shape, lengths.dtype),
        pltpu.SemaphoreType.DMA((2 + len(kept),)),
    ]
    return call(
        taps_kernel, out, [whole(pltpu.HBM)] * (2 + len(kept)),
        4 * window * count * width, 5 << 20, 12, scratch,
    )(*far((taps, lengths, *kept)))


def mix_kernel(begin_col, per, lengths, own, table, gains, spectrum, tables, *refs):
    f_high, f_low, g_high, g_low = parts_of(tables)
    last = len(refs) == 5
    if last:
        first_cols, hidden, inner, normed, chosen = refs
    else:
        hidden, normed, chosen = refs
    lines, _ = table.shape
    count, cols_here = own.shape[1], normed.shape[1]
    window = 2 * count
    half = window // 2
    device = lax.axis_index("row") * lax.axis_size("col") + lax.axis_index("col")
    first = device * count
    base = begin_col if last else 0

    wanted = jnp.maximum(device - 1, 0) * (per + 1) + per
    pick = lax.broadcasted_iota(jnp.int32, (8, lines), 1) == wanted
    digits = dot(jnp.where(pick, 1.0, 0.0).astype(jnp.bfloat16), table[:, : 2 * count])[0:1]
    before = (digits[:, :count] * id_base + digits[:, count:]).astype(jnp.int32)

    rows = table[...].astype(jnp.float32)
    scale = lax.rsqrt(jnp.mean(rows * rows, axis=-1, keepdims=True) + epsilon)
    here = pl.ds(begin_col, cols_here)
    normed[...] = (table[:, here].astype(jnp.float32) * scale * gains[0:1, here]).astype(jnp.bfloat16)
    ids = jnp.concatenate([before, own[...]], axis=1)
    line_of = ids // per * (per + 1) + ids % per
    hit = lax.broadcasted_iota(jnp.int32, (lines, window), 0) == line_of
    chosen[...] = jnp.where(hit, 1.0, 0.0).T.astype(jnp.bfloat16)
    if last:
        hidden[:, :begin_col] = first_cols[...]
    hidden[:, base : base + cols_here] = dot(chosen[count:, :], table[:, here])

    at = lax.broadcasted_iota(jnp.int32, (window, 1), 0) + (first - count)

    def one_user(user, begin):
        end = begin + lengths[user]

        @pl.when(jnp.logical_and(begin < first + count, end > first))
        def _():
            inside = jnp.logical_and(at >= begin, at < end)
            picked = jnp.where(inside, chosen[...].astype(jnp.float32), 0.0).astype(jnp.bfloat16)
            for start in range(0, cols_here, lane_chunk):
                x = dot(picked, normed[:, start : start + lane_chunk]).astype(jnp.bfloat16)
                seen = dot(f_high[...], x) + dot(f_low[...], x)
                x_cos, x_sin = seen[:half], seen[half:]
                cols = pl.ds(begin_col + start, lane_chunk)
                w_cos, w_sin = spectrum[:half, cols], spectrum[half:, cols]
                y = jnp.concatenate(
                    [x_cos * w_cos - x_sin * w_sin, x_cos * w_sin + x_sin * w_cos], axis=0
                )
                y_high = y.astype(jnp.bfloat16)
                y_low = (y - y_high.astype(jnp.float32)).astype(jnp.bfloat16)
                mixed = dot(g_high[...], y_high) + dot(g_high[...], y_low) + dot(g_low[...], y_high)
                cols = pl.ds(base + start, lane_chunk)
                hidden[:, cols] += jnp.where(inside[count:], mixed, 0.0)

        return end

    lax.fori_loop(0, lengths.shape[0], one_user, jnp.int32(0))
    if last:
        mixed = hidden[...]
        scale = lax.rsqrt(jnp.mean(mixed * mixed, axis=-1, keepdims=True) + epsilon)
        inner[...] = (mixed * scale * gains[1:2, :]).astype(jnp.bfloat16)


def mix(begin_col, cols_here, per, lengths, own, table, gains, spectrum, tables, first_cols=None):
    count, (lines, width) = own.shape[1], table.shape
    operands = [lengths, own, table, gains, spectrum, tables]
    if first_cols is None:
        out = shape(count, cols_here, jnp.float32)
    else:
        operands.append(first_cols)
        out = (shape(count, width, jnp.float32), shape(count, width))
    return call(
        functools.partial(mix_kernel, begin_col, per),
        out,
        [whole(pltpu.SMEM)] + [whole()] * (len(operands) - 1),
        2 * cols_here * count * count * 16,
        4 << 20,
        24,
        [pltpu.VMEM((lines, cols_here), jnp.bfloat16), pltpu.VMEM((2 * count, lines), jnp.bfloat16)],
    )(*operands)


def col_route(lane, place):
    pairs = []
    for device in range(lax.axis_size("col")):
        target = place(device // 2)
        if target is not None:
            pairs.append((device, target * 2 + (device % 2 ^ lane)))
    return pairs


def partner(block):
    return lax.ppermute(block, "row", [(i, i ^ 1) for i in range(lax.axis_size("row"))])


def travel(own):
    ends = (0, 3)
    side = col_route(0, lambda p: p ^ 1)
    outward = col_route(0, lambda p: None if p in ends else p ^ 1)
    over_ends = col_route(1, lambda p: p if p in ends else None)
    over_middle = col_route(1, lambda p: None if p in ends else p)
    turn = over_ends + col_route(0, lambda p: None if p in ends else 3 - p)

    def send(block, route):
        return lax.ppermute(block, "col", route)

    b = send(own, side)
    m = send(own, turn)
    a = send(own, over_middle)
    c = send(m, side)
    d = send(b, turn)
    e = send(m, over_middle)
    f = send(d, outward)
    g = send(c, turn)
    cut = own.shape[0] // 2
    t = send(g[:cut], outward)
    u = send(f[cut:], over_ends)
    mine = [b, m, c, d, g, a, f, e, t, u]
    return mine, [partner(block) for block in mine]


def travelled(shares, mine, theirs, depth):
    core = lax.axis_index("row") % 2
    col = lax.axis_index("col")
    lane, place = col % 2, col // 2
    near = jnp.where(place % 2 == 0, place + 1, place - 1)
    middle = jnp.logical_or(place == 1, place == 2)
    at = lambda p, other: p * 2 + (1 - lane if other else lane)
    either = lambda p, q: jnp.where(middle, p, q)
    order = [
        col,
        at(near, False),
        either(at(3 - place, False), at(place, True)),
        either(at(near, True), at(3 - near, False)),
        either(at(3 - near, False), at(near, True)),
        at(3 - near, True),
        either(at(place, True), at(3 - place, False)),
        at(3 - place, True),
    ]
    half = mine[0].shape[1]

    def read(weight, part, start, size):
        rows, cols = slice(weight * depth, (weight + 1) * depth), slice(start, start + size)
        b, m, c, d, g, a, f, e, t, u = mine if part == 0 else theirs
        offset = (core if part == 0 else 1 - core) * half + start
        blocks = [shares[weight][:, pl.ds(pl.multiple_of(offset, size), size)]]
        blocks += [piece[rows, cols] for piece in (b, m, c, d, g)]
        blocks.append(jnp.where(middle, a[rows, cols], f[rows, cols]))
        cut = t.shape[0]
        if rows.stop <= cut:
            end = t[rows, cols]
        elif rows.start >= cut:
            end = u[rows.start - cut : rows.stop - cut, cols]
        else:
            end = jnp.concatenate([t[rows.start :, cols], u[: rows.stop - cut, cols]], axis=0)
        blocks.append(jnp.where(middle, e[rows, cols], end))
        return jnp.concatenate(blocks, axis=0)

    return order, read, core


def feed_kernel(inner, hidden, *refs):
    pieces, (out, ordered, active) = refs[:-3], refs[-3:]
    shares, mine, theirs = pieces[:3], pieces[3:13], pieces[13:]
    depth, half = shares[0].shape[0], mine[0].shape[1]
    order, read, core = travelled(shares, mine, theirs, depth)

    def in_order(source):
        for i, index in enumerate(order):
            cols = pl.ds(pl.multiple_of(index * depth, depth), depth)
            ordered[:, i * depth : (i + 1) * depth] = source[:, cols]

    in_order(inner)
    x = ordered[...]
    for part in range(2):
        for start in range(0, half, lane_chunk):
            gate_sum = dot(x, read(0, part, start, lane_chunk))
            up_sum = dot(x, read(1, part, start, lane_chunk))
            offset = (core if part == 0 else 1 - core) * half + start
            cols = pl.ds(pl.multiple_of(offset, lane_chunk), lane_chunk)
            active[:, cols] = (gate_sum / (1.0 + jnp.exp(-gate_sum)) * up_sum).astype(jnp.bfloat16)
    in_order(active)
    x = ordered[...]
    for part in range(2):
        for start in range(0, half, lane_chunk):
            offset = (core if part == 0 else 1 - core) * half + start
            cols = pl.ds(pl.multiple_of(offset, lane_chunk), lane_chunk)
            out[:, cols] = (hidden[:, cols] + dot(x, read(2, part, start, lane_chunk))).astype(
                jnp.bfloat16
            )


def plain_feed_kernel(inner, hidden, gate, up, down, out, active):
    for start in range(0, gate.shape[1], lane_chunk):
        cols = slice(start, start + lane_chunk)
        gate_sum, up_sum = dot(inner[...], gate[:, cols]), dot(inner[...], up[:, cols])
        active[:, cols] = (gate_sum / (1.0 + jnp.exp(-gate_sum)) * up_sum).astype(jnp.bfloat16)
    for start in range(0, down.shape[1], lane_chunk):
        cols = slice(start, start + lane_chunk)
        out[:, cols] = (hidden[:, cols] + dot(active[...], down[:, cols])).astype(jnp.bfloat16)


def feed(kernel, inner, hidden, pieces, inside, scratch):
    count, width = inner.shape
    return call(
        kernel, shape(count, width), [whole()] * (2 + len(pieces)),
        6 * count * width * inside, 8 << 20, 28, scratch,
    )(inner, hidden, *pieces)


def body(item_ids, user_lengths, catalogue, tap_lengths, conv_taps, norm_gains,
         gate_weight, up_weight, down_weight):
    count, (per, width) = item_ids.shape[0], catalogue.shape
    weights = (gate_weight, up_weight, down_weight)
    shares = [w[0] for w in weights]
    inside = gate_weight.shape[2]
    by_hops = travels()
    if by_hops:
        mine, theirs = travel(pack(*shares))
    sent = greet(item_ids[None], catalogue)
    table = lax.all_to_all(sent, both, 0, 0).reshape(-1, width)
    kept = [jnp.asarray(transform_tables(2 * count, count)), norm_gains[0], item_ids[None]]
    spectrum, tables, gains, ids = taps_spectrum(conv_taps[0], tap_lengths, kept)
    common = (per, user_lengths, ids, table, gains, spectrum, tables)
    first_cols = mix(0, width // 2, *common)
    hidden, inner = mix(width // 2, width // 2, *common, first_cols)
    active = pltpu.VMEM((count, inside), jnp.bfloat16)
    if by_hops:
        pieces, kernel = shares + mine + theirs, feed_kernel
        scratch = [pltpu.VMEM((count, width), jnp.bfloat16), active]
    else:
        pieces = [lax.all_gather(w[0], "col", axis=0, tiled=True) for w in weights]
        kernel, scratch = plain_feed_kernel, [active]
    return feed(kernel, inner, hidden, pieces, inside, scratch)


def travels():
    return lax.axis_size("col") == 8 and lax.axis_size("row") % 2 == 0


def solution(mesh):
    by_device = P(both)
    by_col = P(None, "col", None)
    return jax.shard_map(
        body,
        mesh=mesh,
        in_specs=(by_device, P(), P(both, None), P(), P(), P(), by_col, by_col, by_col),
        out_specs=P(both, None),
        check_vma=False,
    )
```

```python
import functools

import jax
import jax.numpy as jnp
import numpy as np
from jax import lax
from jax.experimental import pallas as pl
from jax.experimental.pallas import tpu as pltpu
from jax.sharding import PartitionSpec as P

epsilon = 1e-06
lane_chunk = 256
mix_chunk = 512
both = ("row", "col")
id_base = 256


def split_bf16(table):
    high = table.astype(jnp.bfloat16)
    low = (table - high.astype(np.float64)).astype(jnp.bfloat16)
    return high, low


def transform_tables(window, out_rows):
    half = window // 2
    angle = 2 * np.pi * np.outer(np.arange(half) + 0.5, np.arange(window)) / window
    forward = np.concatenate([np.cos(angle), np.sin(angle)], axis=0)
    inverse = forward[:, window - out_rows :].T * (2.0 / window)
    (f_high, f_low), (g_high, g_low) = split_bf16(forward), split_bf16(inverse)
    return np.concatenate([f_high, f_low], axis=1), np.concatenate([g_high, g_high, g_low], axis=1)


def dot(a, b):
    return jnp.dot(a, b, preferred_element_type=jnp.float32)


def whole(memory_space=pltpu.VMEM):
    return pl.BlockSpec(memory_space=memory_space)


def shape(rows, width, dtype=jnp.bfloat16):
    return jax.ShapeDtypeStruct((rows, width), dtype)


def far(arrays):
    return [pltpu.with_memory_space_constraint(a, pltpu.HBM) for a in arrays]


def near(arrays):
    return [pltpu.with_memory_space_constraint(a, pltpu.VMEM) for a in arrays]


def call(kernel, out_shape, in_specs, flops, nbytes, limit, scratch=()):
    return pl.pallas_call(
        kernel,
        out_shape=out_shape,
        in_specs=in_specs,
        out_specs=jax.tree.map(lambda _: whole(), out_shape),
        scratch_shapes=list(scratch),
        compiler_params=pltpu.CompilerParams(vmem_limit_bytes=limit << 20),
        cost_estimate=pl.CostEstimate(flops=flops, bytes_accessed=nbytes, transcendentals=0),
    )


def fetch(pairs, sems):
    copies = [pltpu.make_async_copy(a, b, sems.at[i]) for i, (a, b) in enumerate(pairs)]
    for copy in copies:
        copy.start()

    def wait(first=0, end=len(copies)):
        for copy in copies[first:end]:
            copy.wait()

    return wait


def pack_kernel(gate, up, down, own, sems):
    core = lax.axis_index("row") % 2
    depth, half = gate.shape[0], own.shape[1]
    cols = pl.ds(pl.multiple_of(core * half, half), half)
    parts = [(w.at[:, cols], own.at[pl.ds(i * depth, depth)]) for i, w in enumerate((gate, up, down))]
    fetch(parts, sems)()


def pack(gate, up, down):
    depth, width = gate.shape
    return call(
        pack_kernel, pltpu.VMEM((3 * depth, width // 2), gate.dtype), [whole(pltpu.HBM)] * 3, 0, 1 << 20, 4,
        [pltpu.SemaphoreType.DMA((3,))],
    )(*far((gate, up, down)))


def greet_kernel(ids_far, gains_far, rows_far, out, ids, gains, rows, sems):
    wait = fetch([(ids_far, ids), (rows_far, rows), (gains_far, gains)], sems)
    wait(0, 2)
    numbers = ids[...].astype(jnp.float32)
    high = jnp.floor(numbers * (1.0 / id_base))
    digits = [high, numbers - high * id_base]
    digits += [jnp.zeros_like(high)] * (rows.shape[0] - 2)
    digits = jnp.concatenate(digits, axis=0)
    block = jnp.concatenate([rows[...].astype(jnp.float32), digits], axis=1).astype(jnp.bfloat16)

    def one(device, carry):
        out[device] = block
        return carry

    lax.fori_loop(0, out.shape[0], one, 0)
    wait(2)


def greet(ids, gains, rows):
    devices = lax.axis_size("row") * lax.axis_size("col")
    out = jax.ShapeDtypeStruct((devices, rows.shape[0], rows.shape[1] + ids.shape[1]), jnp.bfloat16)
    out = (out, pltpu.VMEM(ids.shape, ids.dtype), pltpu.VMEM(gains.shape, gains.dtype))
    scratch = [pltpu.VMEM(rows.shape, rows.dtype), pltpu.SemaphoreType.DMA((3,))]
    return call(
        greet_kernel, out, [whole(pltpu.HBM)] * 3, 0, 1 << 18, 4, scratch
    )(*far((ids, gains, rows)))


def taps_kernel(after, taps_far, lengths_far, *refs):
    kept, (spectrum, *out), (taps, lengths, sems) = refs[:2], refs[2:5], refs[5:]
    wait = fetch([(taps_far, taps), (lengths_far, lengths), *zip(kept, out)], sems)
    count, window = taps.shape[0], spectrum.shape[0]
    lag = lax.broadcasted_iota(jnp.int32, taps.shape, 0)
    wait(0, 2)
    masked = jnp.where(lag < lengths[...], taps[...].astype(jnp.float32), 0.0).astype(jnp.bfloat16)
    wait(2, 3)
    forward = jnp.concatenate([out[0][:, :count], out[0][:, window : window + count]], axis=1)
    spectrum[...] = dot(forward, jnp.concatenate([masked, masked], axis=0))
    wait(3)


def taps_spectrum(taps, lengths, kept, after):
    window, (count, width) = kept[0].shape[0], taps.shape
    out = [pltpu.VMEM((window, width), jnp.float32)] + [pltpu.VMEM(k.shape, k.dtype) for k in kept]
    scratch = [
        pltpu.VMEM(taps.shape, taps.dtype),
        pltpu.VMEM(lengths.shape, lengths.dtype),
        pltpu.SemaphoreType.DMA((2 + len(kept),)),
    ]
    return call(
        taps_kernel, out, [whole()] + [whole(pltpu.HBM)] * (2 + len(kept)),
        4 * window * count * width, 5 << 20, 8, scratch,
    )(after, *far((taps, lengths, *kept)))


def shelve_kernel(got, own, gains, table, normed, chosen, lines):
    devices, per, _ = got.shape
    items, width = table.shape
    count = own.shape[1]

    group = 8 // per

    def one(index, carry):
        blocks = [got[index * group + i].astype(jnp.float32) for i in range(group)]
        lines[pl.ds(pl.multiple_of(index * 8, 8), 8), :] = jnp.concatenate(blocks, axis=0)
        return carry

    lax.fori_loop(0, devices // group, one, 0, unroll=4)
    rows = lines[:, :width]
    table[...] = rows.astype(jnp.bfloat16)
    scale = lax.rsqrt(jnp.mean(rows * rows, axis=-1, keepdims=True) + epsilon)
    normed[...] = (rows * scale * gains[0:1, :]).astype(jnp.bfloat16)

    device = lax.axis_index("row") * lax.axis_size("col") + lax.axis_index("col")
    wanted = jnp.maximum(device - 1, 0) * per
    line = lax.broadcasted_iota(jnp.int32, (8, items), 1)
    digit = lax.broadcasted_iota(jnp.int32, (8, items), 0)
    pick = jnp.logical_and(line == wanted + digit, digit < 2)
    pick = jnp.where(pick, 1.0, 0.0).astype(jnp.bfloat16)
    digits = dot(pick, lines[:, width:].astype(jnp.bfloat16))
    before = (digits[0:1] * id_base + digits[1:2]).astype(jnp.int32)
    ids = jnp.concatenate([before, own[...]], axis=1)
    hit = lax.broadcasted_iota(jnp.int32, (items, 2 * count), 0) == ids
    chosen[...] = jnp.where(hit, 1.0, 0.0).T.astype(jnp.bfloat16)


def shelve(got, own, gains):
    devices, per, lanes = got.shape
    items, width, count = devices * per, gains.shape[1], own.shape[1]
    rows = pltpu.VMEM((items, width), jnp.bfloat16)
    return call(
        shelve_kernel, (rows, rows, pltpu.VMEM((2 * count, items), jnp.bfloat16)),
        [whole()] * 3, 1 << 20, 1 << 19, 16, [pltpu.VMEM((items, lanes), jnp.float32)],
    )(got, own, gains)


def mix_kernel(begin_col, lengths, table, normed, chosen, gains, spectrum, forward, inverse, *refs):
    last = len(refs) == 3
    first_cols, hidden, inner = refs if last else (None, *refs, None)
    window = chosen.shape[0]
    count, half = window // 2, window // 2
    cols_here = hidden.shape[1] - begin_col if last else hidden.shape[1]
    first = (lax.axis_index("row") * lax.axis_size("col") + lax.axis_index("col")) * count
    base = begin_col if last else 0
    if last:
        hidden[:, :begin_col] = first_cols[...]
    hidden[:, base : base + cols_here] = dot(
        chosen[count:, :], table[:, begin_col : begin_col + cols_here]
    )

    at = lax.broadcasted_iota(jnp.int32, (window, 1), 0) + (first - count)

    def one_user(user, begin):
        end = begin + lengths[user]

        @pl.when(jnp.logical_and(begin < first + count, end > first))
        def _():
            inside = jnp.logical_and(at >= begin, at < end)
            picked = jnp.where(inside, chosen[...].astype(jnp.float32), 0.0).astype(jnp.bfloat16)
            for start in range(0, cols_here, mix_chunk):
                cols = pl.ds(begin_col + start, mix_chunk)
                x = dot(picked, normed[:, cols]).astype(jnp.bfloat16)
                seen = dot(forward[...], jnp.concatenate([x, x], axis=0))
                x_cos, x_sin = seen[:half], seen[half:]
                w_cos, w_sin = spectrum[:half, cols], spectrum[half:, cols]
                y = jnp.concatenate(
                    [x_cos * w_cos - x_sin * w_sin, x_cos * w_sin + x_sin * w_cos], axis=0
                )
                y_high = y.astype(jnp.bfloat16)
                y_low = (y - y_high.astype(jnp.float32)).astype(jnp.bfloat16)
                mixed = dot(inverse[...], jnp.concatenate([y_high, y_low, y_high], axis=0))
                cols = pl.ds(base + start, mix_chunk)
                hidden[:, cols] += jnp.where(inside[count:], mixed, 0.0)

        return end

    lax.fori_loop(0, lengths.shape[0], one_user, jnp.int32(0))
    if last:
        mixed = hidden[...]
        scale = lax.rsqrt(jnp.mean(mixed * mixed, axis=-1, keepdims=True) + epsilon)
        inner[...] = (mixed * scale * gains[1:2, :]).astype(jnp.bfloat16)


def mix(begin_col, cols_here, lengths, looked_up, gains, spectrum, tables, first_cols=None):
    (items, width), window = looked_up[0].shape, looked_up[2].shape[0]
    operands = [lengths, *near(looked_up), gains, spectrum, *near(tables)]
    if first_cols is None:
        out = shape(window // 2, cols_here, jnp.float32)
    else:
        operands.append(first_cols)
        out = (shape(window // 2, width, jnp.float32), shape(window // 2, width))
    return call(
        functools.partial(mix_kernel, begin_col),
        out,
        [whole(pltpu.SMEM)] + [whole()] * (len(operands) - 1),
        8 * cols_here * window * window,
        4 << 20,
        10,
    )(*operands)


def col_route(lane, place):
    pairs = []
    for device in range(lax.axis_size("col")):
        target = place(device // 2)
        if target is not None:
            pairs.append((device, target * 2 + (device % 2 ^ lane)))
    return pairs


def partner(block):
    return lax.ppermute(block, "row", [(i, i ^ 1) for i in range(lax.axis_size("row"))])


def rows_half(block, which):
    cut = block.shape[0] // 2

    def kernel(source, out):
        out[...] = source[which * cut : (which + 1) * cut, :]

    return call(
        kernel, pltpu.VMEM((cut, block.shape[1]), block.dtype), [whole()], 0, 1 << 16, 2
    )(*near([block]))


def travel(own):
    ends = (0, 3)
    side = col_route(0, lambda p: p ^ 1)
    outward = col_route(0, lambda p: None if p in ends else p ^ 1)
    over_ends = col_route(1, lambda p: p if p in ends else None)
    over_middle = col_route(1, lambda p: None if p in ends else p)
    turn = over_ends + col_route(0, lambda p: None if p in ends else 3 - p)

    def send(block, route):
        return lax.ppermute(block, "col", route)

    b = send(own, side)
    m = send(own, turn)
    a = send(own, over_middle)
    c = send(m, side)
    d = send(b, turn)
    e = send(m, over_middle)
    f = send(d, outward)
    g = send(c, turn)
    t = send(rows_half(g, 0), outward)
    u = send(rows_half(f, 1), over_ends)
    mine = [b, m, c, d, g, a, f, e, t, u]
    return mine, [partner(block) for block in mine]


def travelled(shares, mine, theirs, depth):
    core = lax.axis_index("row") % 2
    col = lax.axis_index("col")
    lane, place = col % 2, col // 2
    near = jnp.where(place % 2 == 0, place + 1, place - 1)
    middle = jnp.logical_or(place == 1, place == 2)
    at = lambda p, other: p * 2 + (1 - lane if other else lane)
    either = lambda p, q: jnp.where(middle, p, q)
    order = [
        col,
        at(near, False),
        either(at(3 - place, False), at(place, True)),
        either(at(near, True), at(3 - near, False)),
        either(at(3 - near, False), at(near, True)),
        at(3 - near, True),
        either(at(place, True), at(3 - place, False)),
        at(3 - place, True),
    ]
    half = mine[0].shape[1]

    def read(weight, part, start, size, span):
        rows, cols = slice(weight * depth, (weight + 1) * depth), slice(start, start + size)
        offset = (core if part == 0 else 1 - core) * half + start
        pieces = mine if part == 0 else theirs
        blocks = []
        for i in span:
            if i == 0:
                block = shares[weight][:, pl.ds(pl.multiple_of(offset, size), size)]
            elif i < 6:
                block = pieces[i - 1][rows, cols]
            elif i == 6:
                block = jnp.where(middle, pieces[5][rows, cols], pieces[6][rows, cols])
            else:
                ends = [pieces[8], pieces[9]]
                cut, parts = ends[0].shape[0], []
                for at_row, piece in zip((0, cut), ends):
                    low, high = max(rows.start, at_row) - at_row, min(rows.stop, at_row + cut) - at_row
                    if low < high:
                        parts.append(piece[low:high, cols])
                block = jnp.where(middle, pieces[7][rows, cols], jnp.concatenate(parts, axis=0))
            blocks.append(block)
        return jnp.concatenate(blocks, axis=0)

    def own_cols(part, start, size):
        offset = (core if part == 0 else 1 - core) * half + start
        return pl.ds(pl.multiple_of(offset, size), size)

    def in_order(source, ordered):
        for i, index in enumerate(order):
            cols = pl.ds(pl.multiple_of(index * depth, depth), depth)
            ordered[:, i * depth : (i + 1) * depth] = source[:, cols]

    spots = [(part, start) for part in range(2) for start in range(0, half, lane_chunk)]
    return spots, read, own_cols, in_order


def open_kernel(inner, *refs):
    pieces, (ordered, gate_sums, up_sums) = refs[:-3], refs[-3:]
    shares, mine, theirs = pieces[:2], pieces[2:9], pieces[9:]
    depth = shares[0].shape[0]
    spots, read, _, in_order = travelled(shares, mine, theirs, depth)
    in_order(inner, ordered)
    x = ordered[:, : 7 * depth]
    for i, (part, start) in enumerate(spots):
        cols = slice(i * lane_chunk, (i + 1) * lane_chunk)
        gate_sums[:, cols] = dot(x, read(0, part, start, lane_chunk, range(7)))
        up_sums[:, cols] = dot(x, read(1, part, start, lane_chunk, range(7)))


def close_kernel(hidden, given, gate_sums, up_sums, *refs):
    pieces, (out, ordered, active) = refs[:-3], refs[-3:]
    shares, mine, theirs = pieces[:1], pieces[1:11], pieces[11:]
    depth = shares[0].shape[0]
    spots, read, own_cols, in_order = travelled([None, None, *shares], mine, theirs, depth)
    x = given[:, 7 * depth :]
    for i, (part, start) in enumerate(spots):
        cols = slice(i * lane_chunk, (i + 1) * lane_chunk)
        gate_sum = gate_sums[:, cols] + dot(x, read(0, part, start, lane_chunk, (7,)))
        up_sum = up_sums[:, cols] + dot(x, read(1, part, start, lane_chunk, (7,)))
        active[:, own_cols(part, start, lane_chunk)] = (
            gate_sum / (1.0 + jnp.exp(-gate_sum)) * up_sum
        ).astype(jnp.bfloat16)
    in_order(active, ordered)
    x = ordered[...]
    for part, start in spots:
        cols = own_cols(part, start, lane_chunk)
        out[:, cols] = (hidden[:, cols] + dot(x, read(2, part, start, lane_chunk, range(8)))).astype(
            jnp.bfloat16
        )


def hop_feed(inner, hidden, shares, mine, theirs):
    (count, width), inside = inner.shape, shares[0].shape[1]
    sums = shape(count, inside, jnp.float32)
    early = [*shares[:2], *mine[:7], *theirs[:7]]
    ordered, gate_sums, up_sums = call(
        open_kernel, (shape(count, width), sums, sums), [whole()] * (1 + len(early)),
        4 * count * width * inside, 4 << 20, 8,
    )(inner, *early)
    late = [hidden, ordered, gate_sums, up_sums, shares[2], *mine, *theirs]
    scratch = [pltpu.VMEM((count, inside), jnp.bfloat16), pltpu.VMEM((count, inside), jnp.bfloat16)]
    return call(
        close_kernel, shape(count, width), [whole()] * len(late),
        2 * count * width * inside, 4 << 20, 8, scratch,
    )(*late)


def plain_feed_kernel(inner, hidden, gate, up, down, out, active):
    for start in range(0, gate.shape[1], lane_chunk):
        cols = slice(start, start + lane_chunk)
        gate_sum, up_sum = dot(inner[...], gate[:, cols]), dot(inner[...], up[:, cols])
        active[:, cols] = (gate_sum / (1.0 + jnp.exp(-gate_sum)) * up_sum).astype(jnp.bfloat16)
    for start in range(0, down.shape[1], lane_chunk):
        cols = slice(start, start + lane_chunk)
        out[:, cols] = (hidden[:, cols] + dot(active[...], down[:, cols])).astype(jnp.bfloat16)


def plain_feed(inner, hidden, pieces):
    (count, width), inside = inner.shape, pieces[0].shape[1]
    return call(
        plain_feed_kernel, shape(count, width), [whole()] * 5,
        6 * count * width * inside, 8 << 20, 28, [pltpu.VMEM((count, inside), jnp.bfloat16)],
    )(inner, hidden, *pieces)


def body(item_ids, user_lengths, catalogue, tap_lengths, conv_taps, norm_gains,
         gate_weight, up_weight, down_weight):
    count, width = item_ids.shape[0], catalogue.shape[1]
    weights = (gate_weight, up_weight, down_weight)
    shares = [w[0] for w in weights]
    by_hops = travels()
    if by_hops:
        mine, theirs = travel(pack(*shares))
    sent, ids, gains = greet(item_ids[None], norm_gains[0], catalogue)
    got = lax.all_to_all(sent, both, 0, 0)
    looked_up = shelve(got, ids, gains)
    tables = [*map(jnp.asarray, transform_tables(2 * count, count))]
    spectrum, *tables = taps_spectrum(conv_taps[0], tap_lengths, tables, looked_up[2])
    common = (user_lengths, looked_up, gains, spectrum, tables)
    first_cols = mix(0, width // 2, *common)
    hidden, inner = mix(width // 2, width // 2, *common, first_cols)
    if by_hops:
        return hop_feed(inner, hidden, shares, mine, theirs)
    return plain_feed(
        inner, hidden, [lax.all_gather(w[0], "col", axis=0, tiled=True) for w in weights]
    )


def travels():
    return lax.axis_size("col") == 8 and lax.axis_size("row") % 2 == 0


def solution(mesh):
    by_device = P(both)
    by_col = P(None, "col", None)
    return jax.shard_map(
        body,
        mesh=mesh,
        in_specs=(by_device, P(), P(both, None), P(), P(), P(), by_col, by_col, by_col),
        out_specs=P(both, None),
        check_vma=False,
    )
```

```python
import functools

import jax
import jax.numpy as jnp
import numpy as np
from jax import lax
from jax.experimental import pallas as pl
from jax.experimental.pallas import tpu as pltpu
from jax.sharding import PartitionSpec as P

epsilon = 1e-06
lane_chunk = 256
mix_chunk = 512
both = ("row", "col")
id_base = 256


def split_bf16(table):
    high = table.astype(jnp.bfloat16)
    low = (table - high.astype(np.float64)).astype(jnp.bfloat16)
    return high, low


def transform_tables(window, out_rows):
    half = window // 2
    angle = 2 * np.pi * np.outer(np.arange(half) + 0.5, np.arange(window)) / window
    forward = np.concatenate([np.cos(angle), np.sin(angle)], axis=0)
    inverse = forward[:, window - out_rows :].T * (2.0 / window)
    (f_high, f_low), (g_high, g_low) = split_bf16(forward), split_bf16(inverse)
    return np.concatenate([f_high, f_low], axis=1), np.concatenate([g_high, g_high, g_low], axis=1)


def dot(a, b):
    return jnp.dot(a, b, preferred_element_type=jnp.float32)


def whole(memory_space=pltpu.VMEM):
    return pl.BlockSpec(memory_space=memory_space)


def shape(rows, width, dtype=jnp.bfloat16):
    return jax.ShapeDtypeStruct((rows, width), dtype)


def far(arrays):
    return [pltpu.with_memory_space_constraint(a, pltpu.HBM) for a in arrays]


def near(arrays):
    return [pltpu.with_memory_space_constraint(a, pltpu.VMEM) for a in arrays]


def call(kernel, out_shape, in_specs, flops, nbytes, limit, scratch=()):
    return pl.pallas_call(
        kernel,
        out_shape=out_shape,
        in_specs=in_specs,
        out_specs=jax.tree.map(lambda _: whole(), out_shape),
        scratch_shapes=list(scratch),
        compiler_params=pltpu.CompilerParams(vmem_limit_bytes=limit << 20),
        cost_estimate=pl.CostEstimate(flops=flops, bytes_accessed=nbytes, transcendentals=0),
    )


def fetch(pairs, sems):
    copies = [pltpu.make_async_copy(a, b, sems.at[i]) for i, (a, b) in enumerate(pairs)]
    for copy in copies:
        copy.start()

    def wait(first=0, end=len(copies)):
        for copy in copies[first:end]:
            copy.wait()

    return wait


def pack_kernel(gate, up, down, own, part, sems):
    core = lax.axis_index("row") % 2
    depth, half = gate.shape[0], own.shape[1]
    cols = pl.ds(pl.multiple_of(core * half, half), half)
    parts = [(w.at[:, cols], own.at[pl.ds(i * depth, depth)]) for i, w in enumerate((gate, up, down))]
    fetch(parts, sems)()
    rows = part.shape[0]
    begin = lax.axis_index("row") // 2 % 2 * rows
    part[...] = own[pl.ds(pl.multiple_of(begin, rows), rows), :]


def pack(gate, up, down):
    depth, width = gate.shape
    return call(
        pack_kernel,
        tuple(pltpu.VMEM((rows, width // 2), gate.dtype) for rows in (3 * depth, 3 * depth // 2)),
        [whole(pltpu.HBM)] * 3, 0, 1 << 20, 4,
        [pltpu.SemaphoreType.DMA((3,))],
    )(*far((gate, up, down)))


def greet_kernel(ids_far, gains_far, rows_far, out, ids, gains, rows, sems):
    wait = fetch([(ids_far, ids), (rows_far, rows), (gains_far, gains)], sems)
    wait(0, 2)
    numbers = ids[...].astype(jnp.float32)
    high = jnp.floor(numbers * (1.0 / id_base))
    digits = [high, numbers - high * id_base]
    digits += [jnp.zeros_like(high)] * (rows.shape[0] - 2)
    digits = jnp.concatenate(digits, axis=0)
    block = jnp.concatenate([rows[...].astype(jnp.float32), digits], axis=1).astype(jnp.bfloat16)

    def one(device, carry):
        out[device] = block
        return carry

    lax.fori_loop(0, out.shape[0], one, 0)
    wait(2)


def greet(ids, gains, rows):
    devices = lax.axis_size("row") * lax.axis_size("col")
    out = jax.ShapeDtypeStruct((devices, rows.shape[0], rows.shape[1] + ids.shape[1]), jnp.bfloat16)
    out = (out, pltpu.VMEM(ids.shape, ids.dtype), pltpu.VMEM(gains.shape, gains.dtype))
    scratch = [pltpu.VMEM(rows.shape, rows.dtype), pltpu.SemaphoreType.DMA((3,))]
    return call(
        greet_kernel, out, [whole(pltpu.HBM)] * 3, 0, 1 << 18, 4, scratch
    )(*far((ids, gains, rows)))


def taps_kernel(after, taps_far, lengths_far, *refs):
    kept, (spectrum, *out), (taps, lengths, sems) = refs[:2], refs[2:5], refs[5:]
    wait = fetch([(taps_far, taps), (lengths_far, lengths), *zip(kept, out)], sems)
    count, window = taps.shape[0], spectrum.shape[0]
    lag = lax.broadcasted_iota(jnp.int32, taps.shape, 0)
    wait(0, 2)
    masked = jnp.where(lag < lengths[...], taps[...].astype(jnp.float32), 0.0).astype(jnp.bfloat16)
    wait(2, 3)
    forward = jnp.concatenate([out[0][:, :count], out[0][:, window : window + count]], axis=1)
    spectrum[...] = dot(forward, jnp.concatenate([masked, masked], axis=0))
    wait(3)


def taps_spectrum(taps, lengths, kept, after):
    window, (count, width) = kept[0].shape[0], taps.shape
    out = [pltpu.VMEM((window, width), jnp.float32)] + [pltpu.VMEM(k.shape, k.dtype) for k in kept]
    scratch = [
        pltpu.VMEM(taps.shape, taps.dtype),
        pltpu.VMEM(lengths.shape, lengths.dtype),
        pltpu.SemaphoreType.DMA((2 + len(kept),)),
    ]
    return call(
        taps_kernel, out, [whole()] + [whole(pltpu.HBM)] * (2 + len(kept)),
        4 * window * count * width, 5 << 20, 8, scratch,
    )(after, *far((taps, lengths, *kept)))


def shelve_kernel(got, own, gains, table, normed, chosen, lines):
    devices, per, _ = got.shape
    items, width = table.shape
    count = own.shape[1]

    group = 8 // per

    def one(index, carry):
        blocks = [got[index * group + i].astype(jnp.float32) for i in range(group)]
        lines[pl.ds(pl.multiple_of(index * 8, 8), 8), :] = jnp.concatenate(blocks, axis=0)
        return carry

    lax.fori_loop(0, devices // group, one, 0, unroll=4)
    rows = lines[:, :width]
    table[...] = rows.astype(jnp.bfloat16)
    scale = lax.rsqrt(jnp.mean(rows * rows, axis=-1, keepdims=True) + epsilon)
    normed[...] = (rows * scale * gains[0:1, :]).astype(jnp.bfloat16)

    device = lax.axis_index("row") * lax.axis_size("col") + lax.axis_index("col")
    wanted = jnp.maximum(device - 1, 0) * per
    line = lax.broadcasted_iota(jnp.int32, (8, items), 1)
    digit = lax.broadcasted_iota(jnp.int32, (8, items), 0)
    pick = jnp.logical_and(line == wanted + digit, digit < 2)
    pick = jnp.where(pick, 1.0, 0.0).astype(jnp.bfloat16)
    digits = dot(pick, lines[:, width:].astype(jnp.bfloat16))
    before = (digits[0:1] * id_base + digits[1:2]).astype(jnp.int32)
    ids = jnp.concatenate([before, own[...]], axis=1)
    hit = lax.broadcasted_iota(jnp.int32, (items, 2 * count), 0) == ids
    chosen[...] = jnp.where(hit, 1.0, 0.0).T.astype(jnp.bfloat16)


def shelve(got, own, gains):
    devices, per, lanes = got.shape
    items, width, count = devices * per, gains.shape[1], own.shape[1]
    rows = pltpu.VMEM((items, width), jnp.bfloat16)
    return call(
        shelve_kernel, (rows, rows, pltpu.VMEM((2 * count, items), jnp.bfloat16)),
        [whole()] * 3, 1 << 20, 1 << 19, 16, [pltpu.VMEM((items, lanes), jnp.float32)],
    )(got, own, gains)


def mix_kernel(begin_col, lengths, table, normed, chosen, gains, spectrum, forward, inverse, *refs):
    last = len(refs) == 3
    first_cols, hidden, inner = refs if last else (None, *refs, None)
    window = chosen.shape[0]
    count, half = window // 2, window // 2
    cols_here = hidden.shape[1] - begin_col if last else hidden.shape[1]
    first = (lax.axis_index("row") * lax.axis_size("col") + lax.axis_index("col")) * count
    base = begin_col if last else 0
    if last:
        hidden[:, :begin_col] = first_cols[...]
    hidden[:, base : base + cols_here] = dot(
        chosen[count:, :], table[:, begin_col : begin_col + cols_here]
    )

    at = lax.broadcasted_iota(jnp.int32, (window, 1), 0) + (first - count)

    def one_user(user, begin):
        end = begin + lengths[user]

        @pl.when(jnp.logical_and(begin < first + count, end > first))
        def _():
            inside = jnp.logical_and(at >= begin, at < end)
            picked = jnp.where(inside, chosen[...].astype(jnp.float32), 0.0).astype(jnp.bfloat16)
            for start in range(0, cols_here, mix_chunk):
                cols = pl.ds(begin_col + start, mix_chunk)
                x = dot(picked, normed[:, cols]).astype(jnp.bfloat16)
                seen = dot(forward[...], jnp.concatenate([x, x], axis=0))
                x_cos, x_sin = seen[:half], seen[half:]
                w_cos, w_sin = spectrum[:half, cols], spectrum[half:, cols]
                y = jnp.concatenate(
                    [x_cos * w_cos - x_sin * w_sin, x_cos * w_sin + x_sin * w_cos], axis=0
                )
                y_high = y.astype(jnp.bfloat16)
                y_low = (y - y_high.astype(jnp.float32)).astype(jnp.bfloat16)
                mixed = dot(inverse[...], jnp.concatenate([y_high, y_low, y_high], axis=0))
                cols = pl.ds(base + start, mix_chunk)
                hidden[:, cols] += jnp.where(inside[count:], mixed, 0.0)

        return end

    lax.fori_loop(0, lengths.shape[0], one_user, jnp.int32(0))
    if last:
        mixed = hidden[...]
        scale = lax.rsqrt(jnp.mean(mixed * mixed, axis=-1, keepdims=True) + epsilon)
        inner[...] = (mixed * scale * gains[1:2, :]).astype(jnp.bfloat16)


def mix(begin_col, cols_here, lengths, looked_up, gains, spectrum, tables, first_cols=None):
    (items, width), window = looked_up[0].shape, looked_up[2].shape[0]
    operands = [lengths, *near(looked_up), gains, spectrum, *near(tables)]
    if first_cols is None:
        out = shape(window // 2, cols_here, jnp.float32)
    else:
        operands.append(first_cols)
        out = (shape(window // 2, width, jnp.float32), shape(window // 2, width))
    return call(
        functools.partial(mix_kernel, begin_col),
        out,
        [whole(pltpu.SMEM)] + [whole()] * (len(operands) - 1),
        8 * cols_here * window * window,
        4 << 20,
        10,
    )(*operands)


def col_route(lane, place):
    pairs = []
    for device in range(lax.axis_size("col")):
        target = place(device // 2)
        if target is not None:
            pairs.append((device, target * 2 + (device % 2 ^ lane)))
    return pairs


def partner(block, distance=1):
    return lax.ppermute(
        block, "row", [(i, i ^ distance) for i in range(lax.axis_size("row"))]
    )


def travel(own, part):
    ends = (0, 3)
    side = col_route(0, lambda p: p ^ 1)
    outward = col_route(0, lambda p: None if p in ends else p ^ 1)
    over_middle = col_route(1, lambda p: None if p in ends else p)
    turn = col_route(1, lambda p: p if p in ends else None)
    turn += col_route(0, lambda p: None if p in ends else 3 - p)
    corner = col_route(1, lambda p: 3 - p if p in ends else p)

    def send(block, route):
        return lax.ppermute(block, "col", route)

    b = send(own, side)
    m = send(own, turn)
    k = send(part, corner)
    c = send(m, side)
    d = send(b, turn)
    e = send(m, over_middle)
    kx = partner(k, 2)
    f = send(d, outward)
    g = send(c, turn)
    mine = dict(b=b, m=m, c=c, d=d, k=k, kx=kx, g=g, f=f, e=e)
    return [*mine.values()], [partner(block) for block in mine.values()]


def travelled(shares, mine, theirs, depth):
    core = lax.axis_index("row") % 2
    first_side = lax.axis_index("row") // 2 % 2 == 0
    col = lax.axis_index("col")
    lane, place = col % 2, col // 2
    near = jnp.where(place % 2 == 0, place + 1, place - 1)
    middle = jnp.logical_or(place == 1, place == 2)
    at = lambda p, other: p * 2 + (1 - lane if other else lane)
    either = lambda p, q: jnp.where(middle, p, q)
    order = [
        col,
        at(near, False),
        either(at(3 - place, False), at(place, True)),
        either(at(near, True), at(3 - near, False)),
        either(at(3 - near, False), at(near, True)),
        either(at(place, True), at(3 - place, True)),
        at(3 - near, True),
        either(at(3 - place, True), at(3 - place, False)),
    ]
    half = mine[0].shape[1]

    def read(weight, part, start, size, span):
        rows, cols = slice(weight * depth, (weight + 1) * depth), slice(start, start + size)
        offset = (core if part == 0 else 1 - core) * half + start
        pieces = mine if part == 0 else theirs
        blocks = []
        for i in span:
            if i == 0:
                block = shares[weight][:, pl.ds(pl.multiple_of(offset, size), size)]
            elif i < 5:
                block = pieces[i - 1][rows, cols]
            elif i == 5:
                cut, parts = pieces[4].shape[0], []
                for begin, flip in ((0, False), (cut, True)):
                    low, high = max(rows.start, begin) - begin, min(rows.stop, begin + cut) - begin
                    if low < high:
                        here, there = (piece[low:high, cols] for piece in pieces[4:6])
                        here_first = jnp.logical_not(first_side) if flip else first_side
                        parts.append(jnp.where(here_first, here, there))
                block = jnp.concatenate(parts, axis=0)
            elif i == 6:
                block = pieces[6][rows, cols]
            else:
                block = jnp.where(middle, pieces[8][rows, cols], pieces[7][rows, cols])
            blocks.append(block)
        return jnp.concatenate(blocks, axis=0)

    def own_cols(part, start, size):
        offset = (core if part == 0 else 1 - core) * half + start
        return pl.ds(pl.multiple_of(offset, size), size)

    def in_order(source, ordered):
        for i, index in enumerate(order):
            cols = pl.ds(pl.multiple_of(index * depth, depth), depth)
            ordered[:, i * depth : (i + 1) * depth] = source[:, cols]

    spots = [(part, start) for part in range(2) for start in range(0, half, lane_chunk)]
    return spots, read, own_cols, in_order


def open_kernel(inner, *refs):
    pieces, (ordered, gate_sums, up_sums) = refs[:-3], refs[-3:]
    shares, mine, theirs = pieces[:2], pieces[2:6], pieces[6:]
    depth = shares[0].shape[0]
    spots, read, _, in_order = travelled(shares, mine, theirs, depth)
    in_order(inner, ordered)
    x = ordered[:, : 5 * depth]
    for i, (part, start) in enumerate(spots):
        cols = slice(i * lane_chunk, (i + 1) * lane_chunk)
        gate_sums[:, cols] = dot(x, read(0, part, start, lane_chunk, range(5)))
        up_sums[:, cols] = dot(x, read(1, part, start, lane_chunk, range(5)))


def close_kernel(hidden, given, gate_sums, up_sums, *refs):
    pieces, (out, ordered, active) = refs[:-3], refs[-3:]
    shares, mine, theirs = pieces[:1], pieces[1:10], pieces[10:]
    depth = shares[0].shape[0]
    spots, read, own_cols, in_order = travelled([None, None, *shares], mine, theirs, depth)
    x = given[:, 5 * depth :]
    for i, (part, start) in enumerate(spots):
        cols = slice(i * lane_chunk, (i + 1) * lane_chunk)
        gate_sum = gate_sums[:, cols] + dot(x, read(0, part, start, lane_chunk, (5, 6, 7)))
        up_sum = up_sums[:, cols] + dot(x, read(1, part, start, lane_chunk, (5, 6, 7)))
        active[:, own_cols(part, start, lane_chunk)] = (
            gate_sum / (1.0 + jnp.exp(-gate_sum)) * up_sum
        ).astype(jnp.bfloat16)
    in_order(active, ordered)
    x = ordered[...]
    for part, start in spots:
        cols = own_cols(part, start, lane_chunk)
        out[:, cols] = (hidden[:, cols] + dot(x, read(2, part, start, lane_chunk, range(8)))).astype(
            jnp.bfloat16
        )


def hop_feed(inner, hidden, shares, mine, theirs):
    (count, width), inside = inner.shape, shares[0].shape[1]
    sums = shape(count, inside, jnp.float32)
    early = [*shares[:2], *mine[:4], *theirs[:4]]
    ordered, gate_sums, up_sums = call(
        open_kernel, (shape(count, width), sums, sums), [whole()] * (1 + len(early)),
        4 * count * width * inside, 4 << 20, 8,
    )(inner, *early)
    late = [hidden, ordered, gate_sums, up_sums, shares[2], *mine, *theirs]
    scratch = [pltpu.VMEM((count, inside), jnp.bfloat16), pltpu.VMEM((count, inside), jnp.bfloat16)]
    return call(
        close_kernel, shape(count, width), [whole()] * len(late),
        2 * count * width * inside, 4 << 20, 8, scratch,
    )(*late)


def plain_feed_kernel(inner, hidden, gate, up, down, out, active):
    for start in range(0, gate.shape[1], lane_chunk):
        cols = slice(start, start + lane_chunk)
        gate_sum, up_sum = dot(inner[...], gate[:, cols]), dot(inner[...], up[:, cols])
        active[:, cols] = (gate_sum / (1.0 + jnp.exp(-gate_sum)) * up_sum).astype(jnp.bfloat16)
    for start in range(0, down.shape[1], lane_chunk):
        cols = slice(start, start + lane_chunk)
        out[:, cols] = (hidden[:, cols] + dot(active[...], down[:, cols])).astype(jnp.bfloat16)


def plain_feed(inner, hidden, pieces):
    (count, width), inside = inner.shape, pieces[0].shape[1]
    return call(
        plain_feed_kernel, shape(count, width), [whole()] * 5,
        6 * count * width * inside, 8 << 20, 28, [pltpu.VMEM((count, inside), jnp.bfloat16)],
    )(inner, hidden, *pieces)


def body(item_ids, user_lengths, catalogue, tap_lengths, conv_taps, norm_gains,
         gate_weight, up_weight, down_weight):
    count, width = item_ids.shape[0], catalogue.shape[1]
    weights = (gate_weight, up_weight, down_weight)
    shares = [w[0] for w in weights]
    by_hops = travels()
    if by_hops:
        mine, theirs = travel(*pack(*shares))
    sent, ids, gains = greet(item_ids[None], norm_gains[0], catalogue)
    got = lax.all_to_all(sent, both, 0, 0)
    looked_up = shelve(got, ids, gains)
    tables = [*map(jnp.asarray, transform_tables(2 * count, count))]
    spectrum, *tables = taps_spectrum(conv_taps[0], tap_lengths, tables, looked_up[2])
    common = (user_lengths, looked_up, gains, spectrum, tables)
    first_cols = mix(0, width // 2, *common)
    hidden, inner = mix(width // 2, width // 2, *common, first_cols)
    if by_hops:
        return hop_feed(inner, hidden, shares, mine, theirs)
    return plain_feed(
        inner, hidden, [lax.all_gather(w[0], "col", axis=0, tiled=True) for w in weights]
    )


def travels():
    return lax.axis_size("col") == 8 and lax.axis_size("row") == 4


def solution(mesh):
    by_device = P(both)
    by_col = P(None, "col", None)
    return jax.shard_map(
        body,
        mesh=mesh,
        in_specs=(by_device, P(), P(both, None), P(), P(), P(), by_col, by_col, by_col),
        out_specs=P(both, None),
        check_vma=False,
    )
```

```python
import jax
import jax.numpy as jnp
import numpy as np
from jax import lax
from jax.experimental import pallas as pl
from jax.experimental.pallas import tpu as pltpu
from jax.sharding import PartitionSpec as P

epsilon = 1e-06
lane_chunk = 256
mix_chunk = 1024
both = ("row", "col")
id_base = 256


def split_bf16(table):
    high = table.astype(jnp.bfloat16)
    low = (table - high.astype(np.float64)).astype(jnp.bfloat16)
    return high, low


def transform_tables(window, out_rows):
    half = window // 2
    angle = 2 * np.pi * np.outer(np.arange(half) + 0.5, np.arange(window)) / window
    forward = np.concatenate([np.cos(angle), np.sin(angle)], axis=0)
    inverse = forward[:, window - out_rows :].T * (2.0 / window)
    (f_high, f_low), (g_high, g_low) = split_bf16(forward), split_bf16(inverse)
    return np.concatenate([f_high, f_low], axis=1), np.concatenate([g_high, g_high, g_low], axis=1)


def dot(a, b):
    return jnp.dot(a, b, preferred_element_type=jnp.float32)


def whole(memory_space=pltpu.VMEM):
    return pl.BlockSpec(memory_space=memory_space)


def shape(rows, width, dtype=jnp.bfloat16):
    return jax.ShapeDtypeStruct((rows, width), dtype)


def far(arrays):
    return [pltpu.with_memory_space_constraint(a, pltpu.HBM) for a in arrays]


def near(arrays):
    return [pltpu.with_memory_space_constraint(a, pltpu.VMEM) for a in arrays]


def call(kernel, out_shape, in_specs, flops, nbytes, limit, scratch=()):
    return pl.pallas_call(
        kernel,
        out_shape=out_shape,
        in_specs=in_specs,
        out_specs=jax.tree.map(lambda _: whole(), out_shape),
        scratch_shapes=list(scratch),
        compiler_params=pltpu.CompilerParams(vmem_limit_bytes=limit << 20),
        cost_estimate=pl.CostEstimate(flops=flops, bytes_accessed=nbytes, transcendentals=0),
    )


def fetch(pairs, sems):
    copies = [pltpu.make_async_copy(a, b, sems.at[i]) for i, (a, b) in enumerate(pairs)]
    for copy in copies:
        copy.start()

    def wait(first=0, end=len(copies)):
        for copy in copies[first:end]:
            copy.wait()

    return wait


def pack_kernel(gate, up, down, own, part, sems):
    core = lax.axis_index("row") % 2
    depth, half = gate.shape[0], own.shape[1]
    cols = pl.ds(pl.multiple_of(core * half, half), half)
    parts = [(w.at[:, cols], own.at[pl.ds(i * depth, depth)]) for i, w in enumerate((gate, up, down))]
    fetch(parts, sems)()
    rows = part.shape[0]
    begin = lax.axis_index("row") // 2 % 2 * rows
    part[...] = own[pl.ds(pl.multiple_of(begin, rows), rows), :]


def pack(gate, up, down):
    depth, width = gate.shape
    return call(
        pack_kernel,
        tuple(pltpu.VMEM((rows, width // 2), gate.dtype) for rows in (3 * depth, 3 * depth // 2)),
        [whole(pltpu.HBM)] * 3, 0, 1 << 20, 4,
        [pltpu.SemaphoreType.DMA((3,))],
    )(*far((gate, up, down)))


def greet_kernel(ids_far, gains_far, rows_far, out, ids, gains, rows, sems):
    wait = fetch([(ids_far, ids), (rows_far, rows), (gains_far, gains)], sems)
    wait(0, 2)
    numbers = ids[...].astype(jnp.float32)
    high = jnp.floor(numbers * (1.0 / id_base))
    digits = [high, numbers - high * id_base]
    digits += [jnp.zeros_like(high)] * (rows.shape[0] - 2)
    digits = jnp.concatenate(digits, axis=0)
    block = jnp.concatenate([rows[...].astype(jnp.float32), digits], axis=1).astype(jnp.bfloat16)

    def one(device, carry):
        out[device] = block
        return carry

    lax.fori_loop(0, out.shape[0], one, 0)
    wait(2)


def greet(ids, gains, rows):
    devices = lax.axis_size("row") * lax.axis_size("col")
    out = jax.ShapeDtypeStruct((devices, rows.shape[0], rows.shape[1] + ids.shape[1]), jnp.bfloat16)
    out = (out, pltpu.VMEM(ids.shape, ids.dtype), pltpu.VMEM(gains.shape, gains.dtype))
    scratch = [pltpu.VMEM(rows.shape, rows.dtype), pltpu.SemaphoreType.DMA((3,))]
    return call(
        greet_kernel, out, [whole(pltpu.HBM)] * 3, 0, 1 << 18, 4, scratch
    )(*far((ids, gains, rows)))


def taps_kernel(after, taps_far, lengths_far, *refs):
    kept, (spectrum, *out), (taps, lengths, sems) = refs[:2], refs[2:5], refs[5:]
    wait = fetch([(taps_far, taps), (lengths_far, lengths), *zip(kept, out)], sems)
    count, window = taps.shape[0], spectrum.shape[0]
    lag = lax.broadcasted_iota(jnp.int32, taps.shape, 0)
    wait(0, 2)
    masked = jnp.where(lag < lengths[...], taps[...].astype(jnp.float32), 0.0).astype(jnp.bfloat16)
    wait(2, 3)
    forward = jnp.concatenate([out[0][:, :count], out[0][:, window : window + count]], axis=1)
    spectrum[...] = dot(forward, jnp.concatenate([masked, masked], axis=0))
    wait(3)


def taps_spectrum(taps, lengths, kept, after):
    window, (count, width) = kept[0].shape[0], taps.shape
    out = [pltpu.VMEM((window, width), jnp.float32)] + [pltpu.VMEM(k.shape, k.dtype) for k in kept]
    scratch = [
        pltpu.VMEM(taps.shape, taps.dtype),
        pltpu.VMEM(lengths.shape, lengths.dtype),
        pltpu.SemaphoreType.DMA((2 + len(kept),)),
    ]
    return call(
        taps_kernel, out, [whole()] + [whole(pltpu.HBM)] * (2 + len(kept)),
        4 * window * count * width, 5 << 20, 8, scratch,
    )(after, *far((taps, lengths, *kept)))


def shelve_kernel(got, own, gains, table, normed, chosen, lines):
    devices, per, _ = got.shape
    items, width = table.shape
    count = own.shape[1]

    group = 8 // per

    def one(index, carry):
        blocks = [got[index * group + i].astype(jnp.float32) for i in range(group)]
        lines[pl.ds(pl.multiple_of(index * 8, 8), 8), :] = jnp.concatenate(blocks, axis=0)
        return carry

    lax.fori_loop(0, devices // group, one, 0, unroll=4)
    rows = lines[:, :width]
    table[...] = rows.astype(jnp.bfloat16)
    scale = lax.rsqrt(jnp.mean(rows * rows, axis=-1, keepdims=True) + epsilon)
    normed[...] = (rows * scale * gains[0:1, :]).astype(jnp.bfloat16)

    device = lax.axis_index("row") * lax.axis_size("col") + lax.axis_index("col")
    wanted = jnp.maximum(device - 1, 0) * per
    line = lax.broadcasted_iota(jnp.int32, (8, items), 1)
    digit = lax.broadcasted_iota(jnp.int32, (8, items), 0)
    pick = jnp.logical_and(line == wanted + digit, digit < 2)
    pick = jnp.where(pick, 1.0, 0.0).astype(jnp.bfloat16)
    digits = dot(pick, lines[:, width:].astype(jnp.bfloat16))
    before = (digits[0:1] * id_base + digits[1:2]).astype(jnp.int32)
    ids = jnp.concatenate([before, own[...]], axis=1)
    hit = lax.broadcasted_iota(jnp.int32, (items, 2 * count), 0) == ids
    chosen[...] = jnp.where(hit, 1.0, 0.0).T.astype(jnp.bfloat16)


def shelve(got, own, gains):
    devices, per, lanes = got.shape
    items, width, count = devices * per, gains.shape[1], own.shape[1]
    rows = pltpu.VMEM((items, width), jnp.bfloat16)
    return call(
        shelve_kernel, (rows, rows, pltpu.VMEM((2 * count, items), jnp.bfloat16)),
        [whole()] * 3, 1 << 20, 1 << 19, 16, [pltpu.VMEM((items, lanes), jnp.float32)],
    )(got, own, gains)


def mix_kernel(lengths, given, normed, chosen, gains, spectrum, forward, inverse, hidden, *inner):
    window, width = chosen.shape[0], hidden.shape[1]
    count, half = window // 2, window // 2
    first = (lax.axis_index("row") * lax.axis_size("col") + lax.axis_index("col")) * count
    hidden[...] = given[...] if inner else dot(chosen[count:, :], given[...])

    def add_user(begin, end, skip):
        at = lax.broadcasted_iota(jnp.int32, (window - skip, 1), 0) + (first - count + skip)
        inside = jnp.logical_and(at >= begin, at < end)
        picked = jnp.where(inside, chosen[skip:, :].astype(jnp.float32), 0.0).astype(jnp.bfloat16)
        for start in range(0, width, mix_chunk):
            cols = pl.ds(start, mix_chunk)
            x = dot(picked, normed[:, cols]).astype(jnp.bfloat16)
            table_parts = [forward[:, part + skip : part + window] for part in (0, window)]
            seen = dot(jnp.concatenate(table_parts, axis=1), jnp.concatenate([x, x], axis=0))
            x_cos, x_sin = seen[:half], seen[half:]
            w_cos, w_sin = spectrum[:half, cols], spectrum[half:, cols]
            y = jnp.concatenate(
                [x_cos * w_cos - x_sin * w_sin, x_cos * w_sin + x_sin * w_cos], axis=0
            )
            y_high = y.astype(jnp.bfloat16)
            y_low = (y - y_high.astype(jnp.float32)).astype(jnp.bfloat16)
            mixed = dot(inverse[...], jnp.concatenate([y_high, y_low, y_high], axis=0))
            hidden[:, cols] += jnp.where(inside[count - skip :], mixed, 0.0)

    def one_user(user, begin):
        end = begin + lengths[user]
        here = jnp.logical_and(begin < first + count, end > first)
        if inner:
            pl.when(jnp.logical_and(here, begin >= first))(lambda: add_user(begin, end, count))
        else:
            pl.when(jnp.logical_and(here, begin < first))(lambda: add_user(begin, end, 0))
        return end

    lax.fori_loop(0, lengths.shape[0], one_user, jnp.int32(0))
    if inner:
        mixed = hidden[...]
        scale = lax.rsqrt(jnp.mean(mixed * mixed, axis=-1, keepdims=True) + epsilon)
        inner[0][...] = (mixed * scale * gains[1:2, :]).astype(jnp.bfloat16)


def mix(lengths, given, normed, chosen, gains, spectrum, tables, norm):
    (items, width), window = normed.shape, chosen.shape[0]
    operands = near([given, normed, chosen, gains, spectrum, *tables])
    out = [pltpu.VMEM((window // 2, width), jnp.float32)]
    if norm:
        out.append(pltpu.VMEM((window // 2, width), jnp.bfloat16))
    return call(
        mix_kernel, out, [whole(pltpu.SMEM)] + [whole()] * len(operands),
        8 * width * window * window, 4 << 20, 14,
    )(lengths, *operands)


def col_route(lane, place):
    pairs = []
    for device in range(lax.axis_size("col")):
        target = place(device // 2)
        if target is not None:
            pairs.append((device, target * 2 + (device % 2 ^ lane)))
    return pairs


def partner(block, distance=1):
    return lax.ppermute(
        block, "row", [(i, i ^ distance) for i in range(lax.axis_size("row"))]
    )


def travel(own, part):
    ends = (0, 3)
    side = col_route(0, lambda p: p ^ 1)
    outward = col_route(0, lambda p: None if p in ends else p ^ 1)
    over_middle = col_route(1, lambda p: None if p in ends else p)
    turn = col_route(1, lambda p: p if p in ends else None)
    turn += col_route(0, lambda p: None if p in ends else 3 - p)
    corner = col_route(1, lambda p: 3 - p if p in ends else p)

    def send(block, route):
        return lax.ppermute(block, "col", route)

    b = send(own, side)
    m = send(own, turn)
    k = send(part, corner)
    c = send(m, side)
    d = send(b, turn)
    e = send(m, over_middle)
    kx = partner(k, 2)
    f = send(d, outward)
    g = send(c, turn)
    mine = dict(b=b, m=m, c=c, d=d, k=k, kx=kx, g=g, f=f, e=e)
    return [*mine.values()], [partner(block) for block in mine.values()]


def travelled(shares, mine, theirs, depth):
    core = lax.axis_index("row") % 2
    first_side = lax.axis_index("row") // 2 % 2 == 0
    col = lax.axis_index("col")
    lane, place = col % 2, col // 2
    near = jnp.where(place % 2 == 0, place + 1, place - 1)
    middle = jnp.logical_or(place == 1, place == 2)
    at = lambda p, other: p * 2 + (1 - lane if other else lane)
    either = lambda p, q: jnp.where(middle, p, q)
    order = [
        col,
        at(near, False),
        either(at(3 - place, False), at(place, True)),
        either(at(near, True), at(3 - near, False)),
        either(at(3 - near, False), at(near, True)),
        either(at(place, True), at(3 - place, True)),
        at(3 - near, True),
        either(at(3 - place, True), at(3 - place, False)),
    ]
    half = mine[0].shape[1]

    def read(weight, part, start, size, span):
        rows, cols = slice(weight * depth, (weight + 1) * depth), slice(start, start + size)
        offset = (core if part == 0 else 1 - core) * half + start
        pieces = mine if part == 0 else theirs
        blocks = []
        for i in span:
            if i == 0:
                block = shares[weight][:, pl.ds(pl.multiple_of(offset, size), size)]
            elif i < 5:
                block = pieces[i - 1][rows, cols]
            elif i == 5:
                cut, parts = pieces[4].shape[0], []
                for begin, flip in ((0, False), (cut, True)):
                    low, high = max(rows.start, begin) - begin, min(rows.stop, begin + cut) - begin
                    if low < high:
                        here, there = (piece[low:high, cols] for piece in pieces[4:6])
                        here_first = jnp.logical_not(first_side) if flip else first_side
                        parts.append(jnp.where(here_first, here, there))
                block = jnp.concatenate(parts, axis=0)
            elif i == 6:
                block = pieces[6][rows, cols]
            else:
                block = jnp.where(middle, pieces[8][rows, cols], pieces[7][rows, cols])
            blocks.append(block)
        return jnp.concatenate(blocks, axis=0)

    def own_cols(part, start, size):
        offset = (core if part == 0 else 1 - core) * half + start
        return pl.ds(pl.multiple_of(offset, size), size)

    def in_order(source, ordered):
        for i, index in enumerate(order):
            cols = pl.ds(pl.multiple_of(index * depth, depth), depth)
            ordered[:, i * depth : (i + 1) * depth] = source[:, cols]

    spots = [(part, start) for part in range(2) for start in range(0, half, lane_chunk)]
    return spots, read, own_cols, in_order


def open_kernel(inner, *refs):
    pieces, (ordered, gate_sums, up_sums) = refs[:-3], refs[-3:]
    shares, mine, theirs = pieces[:2], pieces[2:6], pieces[6:]
    depth = shares[0].shape[0]
    spots, read, _, in_order = travelled(shares, mine, theirs, depth)
    in_order(inner, ordered)
    x = ordered[:, : 5 * depth]
    for i, (part, start) in enumerate(spots):
        cols = slice(i * lane_chunk, (i + 1) * lane_chunk)
        gate_sums[:, cols] = dot(x, read(0, part, start, lane_chunk, range(5)))
        up_sums[:, cols] = dot(x, read(1, part, start, lane_chunk, range(5)))


def close_kernel(hidden, given, gate_sums, up_sums, *refs):
    pieces, (out, ordered, active) = refs[:-3], refs[-3:]
    shares, mine, theirs = pieces[:1], pieces[1:10], pieces[10:]
    depth = shares[0].shape[0]
    spots, read, own_cols, in_order = travelled([None, None, *shares], mine, theirs, depth)
    x = given[:, 5 * depth :]
    for i, (part, start) in enumerate(spots):
        cols = slice(i * lane_chunk, (i + 1) * lane_chunk)
        gate_sum = gate_sums[:, cols] + dot(x, read(0, part, start, lane_chunk, (5, 6, 7)))
        up_sum = up_sums[:, cols] + dot(x, read(1, part, start, lane_chunk, (5, 6, 7)))
        active[:, own_cols(part, start, lane_chunk)] = (
            gate_sum / (1.0 + jnp.exp(-gate_sum)) * up_sum
        ).astype(jnp.bfloat16)
    in_order(active, ordered)
    x = ordered[...]
    for part, start in spots:
        cols = own_cols(part, start, lane_chunk)
        out[:, cols] = (hidden[:, cols] + dot(x, read(2, part, start, lane_chunk, range(8)))).astype(
            jnp.bfloat16
        )


def hop_feed(inner, hidden, shares, mine, theirs):
    (count, width), inside = inner.shape, shares[0].shape[1]
    sums = shape(count, inside, jnp.float32)
    early = [*shares[:2], *mine[:4], *theirs[:4]]
    ordered, gate_sums, up_sums = call(
        open_kernel, (shape(count, width), sums, sums), [whole()] * (1 + len(early)),
        4 * count * width * inside, 4 << 20, 8,
    )(inner, *early)
    late = [hidden, ordered, gate_sums, up_sums, shares[2], *mine, *theirs]
    scratch = [pltpu.VMEM((count, inside), jnp.bfloat16), pltpu.VMEM((count, inside), jnp.bfloat16)]
    return call(
        close_kernel, shape(count, width), [whole()] * len(late),
        2 * count * width * inside, 4 << 20, 8, scratch,
    )(*late)


def plain_feed_kernel(inner, hidden, gate, up, down, out, active):
    for start in range(0, gate.shape[1], lane_chunk):
        cols = slice(start, start + lane_chunk)
        gate_sum, up_sum = dot(inner[...], gate[:, cols]), dot(inner[...], up[:, cols])
        active[:, cols] = (gate_sum / (1.0 + jnp.exp(-gate_sum)) * up_sum).astype(jnp.bfloat16)
    for start in range(0, down.shape[1], lane_chunk):
        cols = slice(start, start + lane_chunk)
        out[:, cols] = (hidden[:, cols] + dot(active[...], down[:, cols])).astype(jnp.bfloat16)


def plain_feed(inner, hidden, pieces):
    (count, width), inside = inner.shape, pieces[0].shape[1]
    return call(
        plain_feed_kernel, shape(count, width), [whole()] * 5,
        6 * count * width * inside, 8 << 20, 28, [pltpu.VMEM((count, inside), jnp.bfloat16)],
    )(inner, hidden, *pieces)


def body(item_ids, user_lengths, catalogue, tap_lengths, conv_taps, norm_gains,
         gate_weight, up_weight, down_weight):
    count = item_ids.shape[0]
    weights = (gate_weight, up_weight, down_weight)
    shares = [w[0] for w in weights]
    by_hops = travels()
    if by_hops:
        mine, theirs = travel(*pack(*shares))
    sent, ids, gains = greet(item_ids[None], norm_gains[0], catalogue)
    got = lax.all_to_all(sent, both, 0, 0)
    looked_up = shelve(got, ids, gains)
    tables = [*map(jnp.asarray, transform_tables(2 * count, count))]
    spectrum, *tables = taps_spectrum(conv_taps[0], tap_lengths, tables, looked_up[2])
    table, *looked_up = looked_up
    common = (*looked_up, gains, spectrum, tables)
    (hidden,) = mix(user_lengths, table, *common, False)
    hidden, inner = mix(user_lengths, hidden, *common, True)
    if by_hops:
        return hop_feed(inner, hidden, shares, mine, theirs)
    return plain_feed(
        inner, hidden, [lax.all_gather(w[0], "col", axis=0, tiled=True) for w in weights]
    )


def travels():
    return lax.axis_size("col") == 8 and lax.axis_size("row") == 4


def solution(mesh):
    by_device = P(both)
    by_col = P(None, "col", None)
    return jax.shard_map(
        body,
        mesh=mesh,
        in_specs=(by_device, P(), P(both, None), P(), P(), P(), by_col, by_col, by_col),
        out_specs=P(both, None),
        check_vma=False,
    )
```

```python
import jax
import jax.numpy as jnp
import numpy as np
from jax import lax
from jax.experimental import pallas as pl
from jax.experimental.pallas import tpu as pltpu
from jax.sharding import PartitionSpec as P

epsilon = 1e-06
lane_chunk = 256
mix_chunk = 1024
both = ("row", "col")
id_base = 256


def split_bf16(table):
    high = table.astype(jnp.bfloat16)
    low = (table - high.astype(np.float64)).astype(jnp.bfloat16)
    return high, low


def transform_tables(window, out_rows):
    half = window // 2
    angle = 2 * np.pi * np.outer(np.arange(half) + 0.5, np.arange(window)) / window
    forward = np.concatenate([np.cos(angle), np.sin(angle)], axis=0)
    inverse = forward[:, window - out_rows :].T * (2.0 / window)
    (f_high, f_low), (g_high, g_low) = split_bf16(forward), split_bf16(inverse)
    return np.concatenate([f_high, f_low], axis=1), np.concatenate([g_high, g_high, g_low], axis=1)


def dot(a, b):
    return jnp.dot(a, b, preferred_element_type=jnp.float32)


def whole(memory_space=pltpu.VMEM):
    return pl.BlockSpec(memory_space=memory_space)


def shape(rows, width, dtype=jnp.bfloat16):
    return jax.ShapeDtypeStruct((rows, width), dtype)


def far(arrays):
    return [pltpu.with_memory_space_constraint(a, pltpu.HBM) for a in arrays]


def near(arrays):
    return [pltpu.with_memory_space_constraint(a, pltpu.VMEM) for a in arrays]


def call(kernel, out_shape, in_specs, flops, nbytes, limit, scratch=()):
    return pl.pallas_call(
        kernel,
        out_shape=out_shape,
        in_specs=in_specs,
        out_specs=jax.tree.map(lambda _: whole(), out_shape),
        scratch_shapes=list(scratch),
        compiler_params=pltpu.CompilerParams(vmem_limit_bytes=limit << 20),
        cost_estimate=pl.CostEstimate(flops=flops, bytes_accessed=nbytes, transcendentals=0),
    )


def fetch(pairs, sems):
    copies = [pltpu.make_async_copy(a, b, sems.at[i]) for i, (a, b) in enumerate(pairs)]
    for copy in copies:
        copy.start()

    def wait(first=0, end=len(copies)):
        for copy in copies[first:end]:
            copy.wait()

    return wait


def pack_kernel(gate, up, down, own, part, sems):
    core = lax.axis_index("row") % 2
    depth, half = gate.shape[0], own.shape[1]
    cols = pl.ds(pl.multiple_of(core * half, half), half)
    parts = [(w.at[:, cols], own.at[pl.ds(i * depth, depth)]) for i, w in enumerate((gate, up, down))]
    fetch(parts, sems)()
    rows = part.shape[0]
    begin = lax.axis_index("row") // 2 % 2 * rows
    part[...] = own[pl.ds(pl.multiple_of(begin, rows), rows), :]


def pack(gate, up, down):
    depth, width = gate.shape
    return call(
        pack_kernel,
        tuple(pltpu.VMEM((rows, width // 2), gate.dtype) for rows in (3 * depth, 3 * depth // 2)),
        [whole(pltpu.HBM)] * 3, 0, 1 << 20, 4,
        [pltpu.SemaphoreType.DMA((3,))],
    )(*far((gate, up, down)))


def greet_kernel(ids_far, gains_far, rows_far, out, ids, gains, rows, sems):
    wait = fetch([(ids_far, ids), (rows_far, rows), (gains_far, gains)], sems)
    wait(0, 2)
    numbers = ids[...].astype(jnp.float32)
    high = jnp.floor(numbers * (1.0 / id_base))
    digits = [high, numbers - high * id_base]
    digits += [jnp.zeros_like(high)] * (rows.shape[0] - 2)
    digits = jnp.concatenate(digits, axis=0)
    block = jnp.concatenate([rows[...].astype(jnp.float32), digits], axis=1).astype(jnp.bfloat16)

    def one(device, carry):
        out[device] = block
        return carry

    lax.fori_loop(0, out.shape[0], one, 0)
    wait(2)


def greet(ids, gains, rows):
    devices = lax.axis_size("row") * lax.axis_size("col")
    out = jax.ShapeDtypeStruct((devices, rows.shape[0], rows.shape[1] + ids.shape[1]), jnp.bfloat16)
    out = (out, pltpu.VMEM(ids.shape, ids.dtype), pltpu.VMEM(gains.shape, gains.dtype))
    scratch = [pltpu.VMEM(rows.shape, rows.dtype), pltpu.SemaphoreType.DMA((3,))]
    return call(
        greet_kernel, out, [whole(pltpu.HBM)] * 3, 0, 1 << 18, 4, scratch
    )(*far((ids, gains, rows)))


def taps_kernel(after, taps_far, lengths_far, *refs):
    kept, (spectrum, *out), (taps, lengths, sems) = refs[:2], refs[2:5], refs[5:]
    wait = fetch([(taps_far, taps), (lengths_far, lengths), *zip(kept, out)], sems)
    count, window = taps.shape[0], spectrum.shape[0]
    lag = lax.broadcasted_iota(jnp.int32, taps.shape, 0)
    wait(0, 2)
    masked = jnp.where(lag < lengths[...], taps[...].astype(jnp.float32), 0.0).astype(jnp.bfloat16)
    wait(2, 3)
    forward = jnp.concatenate([out[0][:, :count], out[0][:, window : window + count]], axis=1)
    spectrum[...] = dot(forward, jnp.concatenate([masked, masked], axis=0))
    wait(3)


def taps_spectrum(taps, lengths, kept, after):
    window, (count, width) = kept[0].shape[0], taps.shape
    out = [pltpu.VMEM((window, width), jnp.float32)] + [pltpu.VMEM(k.shape, k.dtype) for k in kept]
    scratch = [
        pltpu.VMEM(taps.shape, taps.dtype),
        pltpu.VMEM(lengths.shape, lengths.dtype),
        pltpu.SemaphoreType.DMA((2 + len(kept),)),
    ]
    return call(
        taps_kernel, out, [whole()] + [whole(pltpu.HBM)] * (2 + len(kept)),
        4 * window * count * width, 5 << 20, 8, scratch,
    )(after, *far((taps, lengths, *kept)))


def shelve_kernel(got, own, gains, table, normed, chosen, lines):
    devices, per, _ = got.shape
    items, width = table.shape
    count = own.shape[1]

    group = 8 // per

    def one(index, carry):
        blocks = [got[index * group + i].astype(jnp.float32) for i in range(group)]
        lines[pl.ds(pl.multiple_of(index * 8, 8), 8), :] = jnp.concatenate(blocks, axis=0)
        return carry

    lax.fori_loop(0, devices // group, one, 0, unroll=4)
    rows = lines[:, :width]
    table[...] = rows.astype(jnp.bfloat16)
    scale = lax.rsqrt(jnp.mean(rows * rows, axis=-1, keepdims=True) + epsilon)
    normed[...] = (rows * scale * gains[0:1, :]).astype(jnp.bfloat16)

    device = lax.axis_index("row") * lax.axis_size("col") + lax.axis_index("col")
    wanted = jnp.maximum(device - 1, 0) * per
    line = lax.broadcasted_iota(jnp.int32, (8, items), 1)
    digit = lax.broadcasted_iota(jnp.int32, (8, items), 0)
    pick = jnp.logical_and(line == wanted + digit, digit < 2)
    pick = jnp.where(pick, 1.0, 0.0).astype(jnp.bfloat16)
    digits = dot(pick, lines[:, width:].astype(jnp.bfloat16))
    before = (digits[0:1] * id_base + digits[1:2]).astype(jnp.int32)
    ids = jnp.concatenate([before, own[...]], axis=1)
    hit = lax.broadcasted_iota(jnp.int32, (items, 2 * count), 0) == ids
    chosen[...] = jnp.where(hit, 1.0, 0.0).T.astype(jnp.bfloat16)


def shelve(got, own, gains):
    devices, per, lanes = got.shape
    items, width, count = devices * per, gains.shape[1], own.shape[1]
    rows = pltpu.VMEM((items, width), jnp.bfloat16)
    return call(
        shelve_kernel, (rows, rows, pltpu.VMEM((2 * count, items), jnp.bfloat16)),
        [whole()] * 3, 1 << 20, 1 << 19, 16, [pltpu.VMEM((items, lanes), jnp.float32)],
    )(got, own, gains)


def mix_kernel(lengths, given, normed, chosen, gains, spectrum, forward, inverse, hidden, *inner):
    window, width = chosen.shape[0], hidden.shape[1]
    count, half = window // 2, window // 2
    first = (lax.axis_index("row") * lax.axis_size("col") + lax.axis_index("col")) * count
    hidden[...] = given[...] if inner else dot(chosen[count:, :], given[...])

    def add_user(begin, end, skip):
        at = lax.broadcasted_iota(jnp.int32, (window - skip, 1), 0) + (first - count + skip)
        inside = jnp.logical_and(at >= begin, at < end)
        picked = jnp.where(inside, chosen[skip:, :].astype(jnp.float32), 0.0).astype(jnp.bfloat16)
        for start in range(0, width, mix_chunk):
            cols = pl.ds(start, mix_chunk)
            x = dot(picked, normed[:, cols]).astype(jnp.bfloat16)
            table_parts = [forward[:, part + skip : part + window] for part in (0, window)]
            seen = dot(jnp.concatenate(table_parts, axis=1), jnp.concatenate([x, x], axis=0))
            x_cos, x_sin = seen[:half], seen[half:]
            w_cos, w_sin = spectrum[:half, cols], spectrum[half:, cols]
            y = jnp.concatenate(
                [x_cos * w_cos - x_sin * w_sin, x_cos * w_sin + x_sin * w_cos], axis=0
            )
            y_high = y.astype(jnp.bfloat16)
            y_low = (y - y_high.astype(jnp.float32)).astype(jnp.bfloat16)
            mixed = dot(inverse[...], jnp.concatenate([y_high, y_low, y_high], axis=0))
            hidden[:, cols] += jnp.where(inside[count - skip :], mixed, 0.0)

    def one_user(user, begin):
        end = begin + lengths[user]
        here = jnp.logical_and(begin < first + count, end > first)
        if inner:
            pl.when(jnp.logical_and(here, begin >= first))(lambda: add_user(begin, end, count))
        else:
            pl.when(jnp.logical_and(here, begin < first))(lambda: add_user(begin, end, 0))
        return end

    lax.fori_loop(0, lengths.shape[0], one_user, jnp.int32(0))
    if inner:
        mixed = hidden[...]
        scale = lax.rsqrt(jnp.mean(mixed * mixed, axis=-1, keepdims=True) + epsilon)
        inner[0][...] = (mixed * scale * gains[1:2, :]).astype(jnp.bfloat16)


def mix(lengths, given, normed, chosen, gains, spectrum, tables, norm):
    (items, width), window = normed.shape, chosen.shape[0]
    operands = near([given, normed, chosen, gains, spectrum, *tables])
    out = [pltpu.VMEM((window // 2, width), jnp.float32)]
    if norm:
        out.append(pltpu.VMEM((window // 2, width), jnp.bfloat16))
    return call(
        mix_kernel, out, [whole(pltpu.SMEM)] + [whole()] * len(operands),
        8 * width * window * window, 4 << 20, 14,
    )(lengths, *operands)


def col_route(lane, place):
    pairs = []
    for device in range(lax.axis_size("col")):
        target = place(device // 2)
        if target is not None:
            pairs.append((device, target * 2 + (device % 2 ^ lane)))
    return pairs


def partner(block, distance=1):
    return lax.ppermute(
        block, "row", [(i, i ^ distance) for i in range(lax.axis_size("row"))]
    )


def travel(own, part):
    ends = (0, 3)
    side = col_route(0, lambda p: p ^ 1)
    outward = col_route(0, lambda p: None if p in ends else p ^ 1)
    over_middle = col_route(1, lambda p: None if p in ends else p)
    turn = col_route(1, lambda p: p if p in ends else None)
    turn += col_route(0, lambda p: None if p in ends else 3 - p)
    corner = col_route(1, lambda p: 3 - p if p in ends else p)

    def send(block, route):
        return lax.ppermute(block, "col", route)

    b = send(own, side)
    m = send(own, turn)
    k = send(part, corner)
    c = send(m, side)
    d = send(b, turn)
    e = send(m, over_middle)
    kx = partner(k, 2)
    f = send(d, outward)
    g = send(c, turn)
    mine = dict(b=b, m=m, c=c, d=d, k=k, kx=kx, g=g, f=f, e=e)
    return [*mine.values()], [partner(block) for block in mine.values()]


def travelled(shares, mine, theirs, depth):
    core = lax.axis_index("row") % 2
    first_side = lax.axis_index("row") // 2 % 2 == 0
    col = lax.axis_index("col")
    lane, place = col % 2, col // 2
    near = jnp.where(place % 2 == 0, place + 1, place - 1)
    middle = jnp.logical_or(place == 1, place == 2)
    at = lambda p, other: p * 2 + (1 - lane if other else lane)
    either = lambda p, q: jnp.where(middle, p, q)
    order = [
        col,
        at(near, False),
        either(at(3 - place, False), at(place, True)),
        either(at(near, True), at(3 - near, False)),
        either(at(3 - near, False), at(near, True)),
        either(at(place, True), at(3 - place, True)),
        at(3 - near, True),
        either(at(3 - place, True), at(3 - place, False)),
    ]
    half = mine[0].shape[1]

    def read(weight, part, start, size, span):
        rows, cols = slice(weight * depth, (weight + 1) * depth), slice(start, start + size)
        offset = (core if part == 0 else 1 - core) * half + start
        pieces = mine if part == 0 else theirs
        blocks = []
        for i in span:
            if i == 0:
                block = shares[weight][:, pl.ds(pl.multiple_of(offset, size), size)]
            elif i < 5:
                block = pieces[i - 1][rows, cols]
            elif i == 5:
                cut, parts = pieces[4].shape[0], []
                for begin, flip in ((0, False), (cut, True)):
                    low, high = max(rows.start, begin) - begin, min(rows.stop, begin + cut) - begin
                    if low < high:
                        here, there = (piece[low:high, cols] for piece in pieces[4:6])
                        here_first = jnp.logical_not(first_side) if flip else first_side
                        parts.append(jnp.where(here_first, here, there))
                block = jnp.concatenate(parts, axis=0)
            elif i == 6:
                block = pieces[6][rows, cols]
            else:
                block = jnp.where(middle, pieces[8][rows, cols], pieces[7][rows, cols])
            blocks.append(block)
        return jnp.concatenate(blocks, axis=0)

    def own_cols(part, start, size):
        offset = (core if part == 0 else 1 - core) * half + start
        return pl.ds(pl.multiple_of(offset, size), size)

    def in_order(source, ordered):
        for i, index in enumerate(order):
            cols = pl.ds(pl.multiple_of(index * depth, depth), depth)
            ordered[:, i * depth : (i + 1) * depth] = source[:, cols]

    spots = [(part, start) for part in range(2) for start in range(0, half, lane_chunk)]
    return spots, read, own_cols, in_order


def activate(gate_sum, up_sum):
    return (gate_sum / (1.0 + jnp.exp(-gate_sum)) * up_sum).astype(jnp.bfloat16)


def open_kernel(inner, *refs):
    pieces, (ordered, own_active, gate_sums, up_sums) = refs[:-4], refs[-4:]
    shares, mine, theirs = pieces[:2], pieces[2:11], pieces[11:]
    depth = shares[0].shape[0]
    spots, read, _, in_order = travelled(shares, mine, theirs, depth)
    in_order(inner, ordered)
    for part, start in spots:
        cols = slice(start, start + lane_chunk)
        span = range(5 if part else 8)
        x = ordered[:, : len(span) * depth]
        gate_sum = dot(x, read(0, part, start, lane_chunk, span))
        up_sum = dot(x, read(1, part, start, lane_chunk, span))
        if part:
            gate_sums[:, cols], up_sums[:, cols] = gate_sum, up_sum
        else:
            own_active[:, cols] = activate(gate_sum, up_sum)


def close_kernel(hidden, given, own_active, gate_sums, up_sums, *refs):
    pieces, (out, ordered, active) = refs[:-3], refs[-3:]
    shares, mine, theirs = pieces[:1], pieces[1:10], pieces[10:]
    depth = shares[0].shape[0]
    spots, read, own_cols, in_order = travelled([None, None, *shares], mine, theirs, depth)
    x = given[:, 5 * depth :]
    for part, start in spots:
        cols = slice(start, start + lane_chunk)
        if part:
            gate_sum = gate_sums[:, cols] + dot(x, read(0, part, start, lane_chunk, (5, 6, 7)))
            up_sum = up_sums[:, cols] + dot(x, read(1, part, start, lane_chunk, (5, 6, 7)))
            units = activate(gate_sum, up_sum)
        else:
            units = own_active[:, cols]
        active[:, own_cols(part, start, lane_chunk)] = units
    in_order(active, ordered)
    x = ordered[...]
    for part, start in spots:
        cols = own_cols(part, start, lane_chunk)
        out[:, cols] = (hidden[:, cols] + dot(x, read(2, part, start, lane_chunk, range(8)))).astype(
            jnp.bfloat16
        )


def hop_feed(inner, hidden, shares, mine, theirs):
    (count, width), inside = inner.shape, shares[0].shape[1]
    sums = shape(count, inside // 2, jnp.float32)
    early = [*shares[:2], *mine, *theirs[:4]]
    opened = call(
        open_kernel, (shape(count, width), shape(count, inside // 2), sums, sums),
        [whole()] * (1 + len(early)), 4 * count * width * inside, 4 << 20, 8,
    )(inner, *early)
    late = [hidden, *opened, shares[2], *mine, *theirs]
    scratch = [pltpu.VMEM((count, inside), jnp.bfloat16), pltpu.VMEM((count, inside), jnp.bfloat16)]
    return call(
        close_kernel, shape(count, width), [whole()] * len(late),
        2 * count * width * inside, 4 << 20, 8, scratch,
    )(*late)


def plain_feed_kernel(inner, hidden, gate, up, down, out, active):
    for start in range(0, gate.shape[1], lane_chunk):
        cols = slice(start, start + lane_chunk)
        gate_sum, up_sum = dot(inner[...], gate[:, cols]), dot(inner[...], up[:, cols])
        active[:, cols] = (gate_sum / (1.0 + jnp.exp(-gate_sum)) * up_sum).astype(jnp.bfloat16)
    for start in range(0, down.shape[1], lane_chunk):
        cols = slice(start, start + lane_chunk)
        out[:, cols] = (hidden[:, cols] + dot(active[...], down[:, cols])).astype(jnp.bfloat16)


def plain_feed(inner, hidden, pieces):
    (count, width), inside = inner.shape, pieces[0].shape[1]
    return call(
        plain_feed_kernel, shape(count, width), [whole()] * 5,
        6 * count * width * inside, 8 << 20, 28, [pltpu.VMEM((count, inside), jnp.bfloat16)],
    )(inner, hidden, *pieces)


def body(item_ids, user_lengths, catalogue, tap_lengths, conv_taps, norm_gains,
         gate_weight, up_weight, down_weight):
    count = item_ids.shape[0]
    weights = (gate_weight, up_weight, down_weight)
    shares = [w[0] for w in weights]
    by_hops = travels()
    if by_hops:
        mine, theirs = travel(*pack(*shares))
    sent, ids, gains = greet(item_ids[None], norm_gains[0], catalogue)
    got = lax.all_to_all(sent, both, 0, 0)
    looked_up = shelve(got, ids, gains)
    tables = [*map(jnp.asarray, transform_tables(2 * count, count))]
    spectrum, *tables = taps_spectrum(conv_taps[0], tap_lengths, tables, looked_up[2])
    table, *looked_up = looked_up
    common = (*looked_up, gains, spectrum, tables)
    (hidden,) = mix(user_lengths, table, *common, False)
    hidden, inner = mix(user_lengths, hidden, *common, True)
    if by_hops:
        return hop_feed(inner, hidden, shares, mine, theirs)
    return plain_feed(
        inner, hidden, [lax.all_gather(w[0], "col", axis=0, tiled=True) for w in weights]
    )


def travels():
    return lax.axis_size("col") == 8 and lax.axis_size("row") == 4


def solution(mesh):
    by_device = P(both)
    by_col = P(None, "col", None)
    return jax.shard_map(
        body,
        mesh=mesh,
        in_specs=(by_device, P(), P(both, None), P(), P(), P(), by_col, by_col, by_col),
        out_specs=P(both, None),
        check_vma=False,
    )
```

```python
import jax
import jax.numpy as jnp
import numpy as np
from jax import lax
from jax.experimental import pallas as pl
from jax.experimental.pallas import tpu as pltpu
from jax.sharding import PartitionSpec as P

epsilon = 1e-06
lane_chunk = 256
mix_chunk = 1024
both = ("row", "col")
id_base = 256


def split_bf16(table):
    high = table.astype(jnp.bfloat16)
    low = (table - high.astype(np.float64)).astype(jnp.bfloat16)
    return high, low


def transform_tables(window, out_rows):
    half = window // 2
    angle = 2 * np.pi * np.outer(np.arange(half) + 0.5, np.arange(window)) / window
    forward = np.concatenate([np.cos(angle), np.sin(angle)], axis=0)
    inverse = forward[:, window - out_rows :].T * (2.0 / window)
    (f_high, f_low), (g_high, g_low) = split_bf16(forward), split_bf16(inverse)
    return np.concatenate([f_high, f_low], axis=1), np.concatenate([g_high, g_high, g_low], axis=1)


def dot(a, b):
    return jnp.dot(a, b, preferred_element_type=jnp.float32)


def whole(memory_space=pltpu.VMEM):
    return pl.BlockSpec(memory_space=memory_space)


def shape(rows, width, dtype=jnp.bfloat16):
    return jax.ShapeDtypeStruct((rows, width), dtype)


def far(arrays):
    return [pltpu.with_memory_space_constraint(a, pltpu.HBM) for a in arrays]


def near(arrays):
    return [pltpu.with_memory_space_constraint(a, pltpu.VMEM) for a in arrays]


def call(kernel, out_shape, in_specs, flops, nbytes, limit, scratch=(), out_specs=None):
    return pl.pallas_call(
        kernel,
        out_shape=out_shape,
        in_specs=in_specs,
        out_specs=out_specs or jax.tree.map(lambda _: whole(), out_shape),
        scratch_shapes=list(scratch),
        compiler_params=pltpu.CompilerParams(vmem_limit_bytes=limit << 20),
        cost_estimate=pl.CostEstimate(flops=flops, bytes_accessed=nbytes, transcendentals=0),
    )


def fetch(pairs, sems):
    copies = [pltpu.make_async_copy(a, b, sems.at[i]) for i, (a, b) in enumerate(pairs)]
    for copy in copies:
        copy.start()

    def wait(first=0, end=len(copies)):
        for copy in copies[first:end]:
            copy.wait()

    return wait


def pack_kernel(gate, up, down, own, part, sems):
    core = lax.axis_index("row") % 2
    depth, half = gate.shape[0], own.shape[1]
    cols = pl.ds(pl.multiple_of(core * half, half), half)
    parts = [(w.at[:, cols], own.at[pl.ds(i * depth, depth)]) for i, w in enumerate((gate, up, down))]
    fetch(parts, sems)()
    rows = part.shape[0]
    begin = lax.axis_index("row") // 2 % 2 * rows
    part[...] = own[pl.ds(pl.multiple_of(begin, rows), rows), :]


def pack(gate, up, down):
    depth, width = gate.shape
    return call(
        pack_kernel,
        tuple(pltpu.VMEM((rows, width // 2), gate.dtype) for rows in (3 * depth, 3 * depth // 2)),
        [whole(pltpu.HBM)] * 3, 0, 1 << 20, 4,
        [pltpu.SemaphoreType.DMA((3,))],
    )(*far((gate, up, down)))


def greet_kernel(ids_far, gains_far, rows_far, out, ids, gains, rows, sems):
    wait = fetch([(ids_far, ids), (rows_far, rows), (gains_far, gains)], sems)
    wait(0, 2)
    numbers = ids[...].astype(jnp.float32)
    high = jnp.floor(numbers * (1.0 / id_base))
    digits = [high, numbers - high * id_base]
    digits += [jnp.zeros_like(high)] * (rows.shape[0] - 2)
    digits = jnp.concatenate(digits, axis=0)
    block = jnp.concatenate([rows[...].astype(jnp.float32), digits], axis=1).astype(jnp.bfloat16)

    def one(device, carry):
        out[device] = block
        return carry

    lax.fori_loop(0, out.shape[0], one, 0)
    wait(2)


def greet(ids, gains, rows):
    devices = lax.axis_size("row") * lax.axis_size("col")
    out = jax.ShapeDtypeStruct((devices, rows.shape[0], rows.shape[1] + ids.shape[1]), jnp.bfloat16)
    out = (out, pltpu.VMEM(ids.shape, ids.dtype), pltpu.VMEM(gains.shape, gains.dtype))
    scratch = [pltpu.VMEM(rows.shape, rows.dtype), pltpu.SemaphoreType.DMA((3,))]
    return call(
        greet_kernel, out, [whole(pltpu.HBM)] * 3, 0, 1 << 18, 4, scratch
    )(*far((ids, gains, rows)))


def taps_kernel(after, taps_far, lengths_far, *refs):
    kept, (spectrum, *out), (taps, lengths, sems) = refs[:2], refs[2:5], refs[5:]
    wait = fetch([(taps_far, taps), (lengths_far, lengths), *zip(kept, out)], sems)
    count, window = taps.shape[0], spectrum.shape[0]
    lag = lax.broadcasted_iota(jnp.int32, taps.shape, 0)
    wait(0, 2)
    masked = jnp.where(lag < lengths[...], taps[...].astype(jnp.float32), 0.0).astype(jnp.bfloat16)
    wait(2, 3)
    forward = jnp.concatenate([out[0][:, :count], out[0][:, window : window + count]], axis=1)
    spectrum[...] = dot(forward, jnp.concatenate([masked, masked], axis=0))
    wait(3)


def taps_spectrum(taps, lengths, kept, after):
    window, (count, width) = kept[0].shape[0], taps.shape
    out = [pltpu.VMEM((window, width), jnp.float32)] + [pltpu.VMEM(k.shape, k.dtype) for k in kept]
    scratch = [
        pltpu.VMEM(taps.shape, taps.dtype),
        pltpu.VMEM(lengths.shape, lengths.dtype),
        pltpu.SemaphoreType.DMA((2 + len(kept),)),
    ]
    return call(
        taps_kernel, out, [whole()] + [whole(pltpu.HBM)] * (2 + len(kept)),
        4 * window * count * width, 5 << 20, 8, scratch,
    )(after, *far((taps, lengths, *kept)))


def shelve_kernel(got, own, gains, table, normed, chosen, lines):
    devices, per, _ = got.shape
    items, width = table.shape
    count = own.shape[1]

    group = 8 // per

    def one(index, carry):
        blocks = [got[index * group + i].astype(jnp.float32) for i in range(group)]
        lines[pl.ds(pl.multiple_of(index * 8, 8), 8), :] = jnp.concatenate(blocks, axis=0)
        return carry

    lax.fori_loop(0, devices // group, one, 0, unroll=4)
    rows = lines[:, :width]
    table[...] = rows.astype(jnp.bfloat16)
    scale = lax.rsqrt(jnp.mean(rows * rows, axis=-1, keepdims=True) + epsilon)
    normed[...] = (rows * scale * gains[0:1, :]).astype(jnp.bfloat16)

    device = lax.axis_index("row") * lax.axis_size("col") + lax.axis_index("col")
    wanted = jnp.maximum(device - 1, 0) * per
    line = lax.broadcasted_iota(jnp.int32, (8, items), 1)
    digit = lax.broadcasted_iota(jnp.int32, (8, items), 0)
    pick = jnp.logical_and(line == wanted + digit, digit < 2)
    pick = jnp.where(pick, 1.0, 0.0).astype(jnp.bfloat16)
    digits = dot(pick, lines[:, width:].astype(jnp.bfloat16))
    before = (digits[0:1] * id_base + digits[1:2]).astype(jnp.int32)
    ids = jnp.concatenate([before, own[...]], axis=1)
    hit = lax.broadcasted_iota(jnp.int32, (items, 2 * count), 0) == ids
    chosen[...] = jnp.where(hit, 1.0, 0.0).T.astype(jnp.bfloat16)


def shelve(got, own, gains):
    devices, per, lanes = got.shape
    items, width, count = devices * per, gains.shape[1], own.shape[1]
    rows = pltpu.VMEM((items, width), jnp.bfloat16)
    return call(
        shelve_kernel, (rows, rows, pltpu.VMEM((2 * count, items), jnp.bfloat16)),
        [whole()] * 3, 1 << 20, 1 << 19, 16, [pltpu.VMEM((items, lanes), jnp.float32)],
    )(got, own, gains)


def mix_kernel(lengths, given, normed, chosen, gains, spectrum, forward, inverse, hidden, *inner):
    window, width = chosen.shape[0], hidden.shape[1]
    count, half = window // 2, window // 2
    first = (lax.axis_index("row") * lax.axis_size("col") + lax.axis_index("col")) * count
    hidden[...] = given[...] if inner else dot(chosen[count:, :], given[...])

    def add_user(begin, end, skip):
        at = lax.broadcasted_iota(jnp.int32, (window - skip, 1), 0) + (first - count + skip)
        inside = jnp.logical_and(at >= begin, at < end)
        picked = jnp.where(inside, chosen[skip:, :].astype(jnp.float32), 0.0).astype(jnp.bfloat16)
        for start in range(0, width, mix_chunk):
            cols = pl.ds(start, mix_chunk)
            x = dot(picked, normed[:, cols]).astype(jnp.bfloat16)
            table_parts = [forward[:, part + skip : part + window] for part in (0, window)]
            seen = dot(jnp.concatenate(table_parts, axis=1), jnp.concatenate([x, x], axis=0))
            x_cos, x_sin = seen[:half], seen[half:]
            w_cos, w_sin = spectrum[:half, cols], spectrum[half:, cols]
            y = jnp.concatenate(
                [x_cos * w_cos - x_sin * w_sin, x_cos * w_sin + x_sin * w_cos], axis=0
            )
            y_high = y.astype(jnp.bfloat16)
            y_low = (y - y_high.astype(jnp.float32)).astype(jnp.bfloat16)
            mixed = dot(inverse[...], jnp.concatenate([y_high, y_low, y_high], axis=0))
            hidden[:, cols] += jnp.where(inside[count - skip :], mixed, 0.0)

    def one_user(user, begin):
        end = begin + lengths[user]
        here = jnp.logical_and(begin < first + count, end > first)
        if inner:
            pl.when(jnp.logical_and(here, begin >= first))(lambda: add_user(begin, end, count))
        else:
            pl.when(jnp.logical_and(here, begin < first))(lambda: add_user(begin, end, 0))
        return end

    lax.fori_loop(0, lengths.shape[0], one_user, jnp.int32(0))
    if inner:
        mixed = hidden[...]
        scale = lax.rsqrt(jnp.mean(mixed * mixed, axis=-1, keepdims=True) + epsilon)
        inner[0][...] = (mixed * scale * gains[1:2, :]).astype(jnp.bfloat16)


def mix(lengths, given, normed, chosen, gains, spectrum, tables, norm):
    (items, width), window = normed.shape, chosen.shape[0]
    operands = near([given, normed, chosen, gains, spectrum, *tables])
    out = [pltpu.VMEM((window // 2, width), jnp.float32)]
    if norm:
        out.append(pltpu.VMEM((window // 2, width), jnp.bfloat16))
    return call(
        mix_kernel, out, [whole(pltpu.SMEM)] + [whole()] * len(operands),
        8 * width * window * window, 4 << 20, 14,
    )(lengths, *operands)


def col_route(lane, place):
    pairs = []
    for device in range(lax.axis_size("col")):
        target = place(device // 2)
        if target is not None:
            pairs.append((device, target * 2 + (device % 2 ^ lane)))
    return pairs


def partner(block, distance=1):
    return lax.ppermute(
        block, "row", [(i, i ^ distance) for i in range(lax.axis_size("row"))]
    )


def travel(own, part):
    ends = (0, 3)
    side = col_route(0, lambda p: p ^ 1)
    outward = col_route(0, lambda p: None if p in ends else p ^ 1)
    over_middle = col_route(1, lambda p: None if p in ends else p)
    turn = col_route(1, lambda p: p if p in ends else None)
    turn += col_route(0, lambda p: None if p in ends else 3 - p)
    corner = col_route(1, lambda p: 3 - p if p in ends else p)

    def send(block, route):
        return lax.ppermute(block, "col", route)

    b = send(own, side)
    m = send(own, turn)
    k = send(part, corner)
    c = send(m, side)
    d = send(b, turn)
    e = send(m, over_middle)
    kx = partner(k, 2)
    f = send(d, outward)
    g = send(c, turn)
    mine = dict(b=b, m=m, c=c, d=d, k=k, kx=kx, g=g, f=f, e=e)
    return [*mine.values()], [partner(block) for block in mine.values()]


def travelled(shares, mine, theirs, depth):
    core = lax.axis_index("row") % 2
    first_side = lax.axis_index("row") // 2 % 2 == 0
    col = lax.axis_index("col")
    lane, place = col % 2, col // 2
    near = jnp.where(place % 2 == 0, place + 1, place - 1)
    middle = jnp.logical_or(place == 1, place == 2)
    at = lambda p, other: p * 2 + (1 - lane if other else lane)
    either = lambda p, q: jnp.where(middle, p, q)
    order = [
        col,
        at(near, False),
        either(at(3 - place, False), at(place, True)),
        either(at(near, True), at(3 - near, False)),
        either(at(3 - near, False), at(near, True)),
        either(at(place, True), at(3 - place, True)),
        at(3 - near, True),
        either(at(3 - place, True), at(3 - place, False)),
    ]
    half = mine[0].shape[1]

    def read(weight, part, start, size, span):
        rows, cols = slice(weight * depth, (weight + 1) * depth), slice(start, start + size)
        offset = (core if part == 0 else 1 - core) * half + start
        pieces = mine if part == 0 else theirs
        blocks = []
        for i in span:
            if i == 0:
                block = shares[weight][:, pl.ds(pl.multiple_of(offset, size), size)]
            elif i < 5:
                block = pieces[i - 1][rows, cols]
            elif i == 5:
                cut, parts = pieces[4].shape[0], []
                for begin, flip in ((0, False), (cut, True)):
                    low, high = max(rows.start, begin) - begin, min(rows.stop, begin + cut) - begin
                    if low < high:
                        here, there = (piece[low:high, cols] for piece in pieces[4:6])
                        here_first = jnp.logical_not(first_side) if flip else first_side
                        parts.append(jnp.where(here_first, here, there))
                block = jnp.concatenate(parts, axis=0)
            elif i == 6:
                block = pieces[6][rows, cols]
            else:
                block = jnp.where(middle, pieces[8][rows, cols], pieces[7][rows, cols])
            blocks.append(block)
        return jnp.concatenate(blocks, axis=0)

    def own_cols(part, start, size):
        offset = (core if part == 0 else 1 - core) * half + start
        return pl.ds(pl.multiple_of(offset, size), size)

    def in_order(source, ordered):
        for i, index in enumerate(order):
            cols = pl.ds(pl.multiple_of(index * depth, depth), depth)
            ordered[:, i * depth : (i + 1) * depth] = source[:, cols]

    spots = [(part, start) for part in range(2) for start in range(0, half, lane_chunk)]
    return spots, read, own_cols, in_order


def activate(gate_sum, up_sum):
    return (gate_sum / (1.0 + jnp.exp(-gate_sum)) * up_sum).astype(jnp.bfloat16)


def open_kernel(inner, *refs):
    pieces, (ordered, own_active, gate_sums, up_sums) = refs[:-4], refs[-4:]
    shares, mine, theirs = pieces[:2], pieces[2:11], pieces[11:]
    depth = shares[0].shape[0]
    spots, read, _, in_order = travelled(shares, mine, theirs, depth)
    in_order(inner, ordered)
    for part, start in spots:
        cols = slice(start, start + lane_chunk)
        span = range(5 if part else 8)
        x = ordered[:, : len(span) * depth]
        gate_sum = dot(x, read(0, part, start, lane_chunk, span))
        up_sum = dot(x, read(1, part, start, lane_chunk, span))
        if part:
            gate_sums[:, cols], up_sums[:, cols] = gate_sum, up_sum
        else:
            own_active[:, cols] = activate(gate_sum, up_sum)


def close_kernel(hidden, given, own_active, gate_sums, up_sums, *refs):
    pieces, (out_far, out, ordered, active, sems) = refs[:-5], refs[-5:]
    shares, mine, theirs = pieces[:1], pieces[1:10], pieces[10:]
    depth = shares[0].shape[0]
    spots, read, own_cols, in_order = travelled([None, None, *shares], mine, theirs, depth)
    x = given[:, 5 * depth :]
    for part, start in spots:
        cols = slice(start, start + lane_chunk)
        if part:
            gate_sum = gate_sums[:, cols] + dot(x, read(0, part, start, lane_chunk, (5, 6, 7)))
            up_sum = up_sums[:, cols] + dot(x, read(1, part, start, lane_chunk, (5, 6, 7)))
            units = activate(gate_sum, up_sum)
        else:
            units = own_active[:, cols]
        active[:, own_cols(part, start, lane_chunk)] = units
    in_order(active, ordered)
    x = ordered[...]
    copies = []
    for i, (part, start) in enumerate(spots):
        cols = own_cols(part, start, lane_chunk)
        out[:, cols] = (hidden[:, cols] + dot(x, read(2, part, start, lane_chunk, range(8)))).astype(
            jnp.bfloat16
        )
        copies.append(pltpu.make_async_copy(out.at[:, cols], out_far.at[:, cols], sems.at[i]))
        copies[-1].start()
    for copy in copies:
        copy.wait()


def hop_feed(inner, hidden, shares, mine, theirs):
    (count, width), inside = inner.shape, shares[0].shape[1]
    sums = shape(count, inside // 2, jnp.float32)
    early = [*shares[:2], *mine, *theirs[:4]]
    opened = call(
        open_kernel, (shape(count, width), shape(count, inside // 2), sums, sums),
        [whole()] * (1 + len(early)), 4 * count * width * inside, 4 << 20, 8,
    )(inner, *early)
    late = [hidden, *opened, shares[2], *mine, *theirs]
    scratch = [pltpu.VMEM((count, width), jnp.bfloat16)]
    scratch += [pltpu.VMEM((count, inside), jnp.bfloat16)] * 2
    scratch.append(pltpu.SemaphoreType.DMA((width // lane_chunk,)))
    return call(
        close_kernel, shape(count, width), [whole()] * len(late),
        2 * count * width * inside, 4 << 20, 8, scratch, whole(pltpu.HBM),
    )(*late)


def plain_feed_kernel(inner, hidden, gate, up, down, out, active):
    for start in range(0, gate.shape[1], lane_chunk):
        cols = slice(start, start + lane_chunk)
        gate_sum, up_sum = dot(inner[...], gate[:, cols]), dot(inner[...], up[:, cols])
        active[:, cols] = (gate_sum / (1.0 + jnp.exp(-gate_sum)) * up_sum).astype(jnp.bfloat16)
    for start in range(0, down.shape[1], lane_chunk):
        cols = slice(start, start + lane_chunk)
        out[:, cols] = (hidden[:, cols] + dot(active[...], down[:, cols])).astype(jnp.bfloat16)


def plain_feed(inner, hidden, pieces):
    (count, width), inside = inner.shape, pieces[0].shape[1]
    return call(
        plain_feed_kernel, shape(count, width), [whole()] * 5,
        6 * count * width * inside, 8 << 20, 28, [pltpu.VMEM((count, inside), jnp.bfloat16)],
    )(inner, hidden, *pieces)


def body(item_ids, user_lengths, catalogue, tap_lengths, conv_taps, norm_gains,
         gate_weight, up_weight, down_weight):
    count = item_ids.shape[0]
    weights = (gate_weight, up_weight, down_weight)
    shares = [w[0] for w in weights]
    by_hops = travels()
    if by_hops:
        mine, theirs = travel(*pack(*shares))
    sent, ids, gains = greet(item_ids[None], norm_gains[0], catalogue)
    got = lax.all_to_all(sent, both, 0, 0)
    looked_up = shelve(got, ids, gains)
    tables = [*map(jnp.asarray, transform_tables(2 * count, count))]
    spectrum, *tables = taps_spectrum(conv_taps[0], tap_lengths, tables, looked_up[2])
    table, *looked_up = looked_up
    common = (*looked_up, gains, spectrum, tables)
    (hidden,) = mix(user_lengths, table, *common, False)
    hidden, inner = mix(user_lengths, hidden, *common, True)
    if by_hops:
        return hop_feed(inner, hidden, shares, mine, theirs)
    return plain_feed(
        inner, hidden, [lax.all_gather(w[0], "col", axis=0, tiled=True) for w in weights]
    )


def travels():
    return lax.axis_size("col") == 8 and lax.axis_size("row") == 4


def solution(mesh):
    by_device = P(both)
    by_col = P(None, "col", None)
    return jax.shard_map(
        body,
        mesh=mesh,
        in_specs=(by_device, P(), P(both, None), P(), P(), P(), by_col, by_col, by_col),
        out_specs=P(both, None),
        check_vma=False,
    )
```
